512 devices in a mesh: seq: 64 (over y_lo, x, z), head: 8 (over y_hi, core).
Axes of the slice: x: 4, y: 8 (y_hi: 4, y_lo: 2; y = y_hi * 2 + y_lo), z: 8, core: 2. Of those that a mesh axis runs over, the one named last changes fastest.
Arguments:
- queries: bfloat16 [16384, 3072], P(('seq', 'head')), may hold values from -6 to 6
- keys: bfloat16 [16384, 3072], P('seq', 'head'), may hold values from -6 to 6
- values: bfloat16 [16384, 3072], P('seq', 'head'), may hold values from -6 to 6
- window: int32 [64, 27], P('seq'), may hold values from -1 to 63, as said below
- out_weight: bfloat16 [3072, 6144], P('seq', 'head'), may hold values from -0.109375 to 0.109375
Outputs:
- projected: bfloat16 [16384, 6144], P('seq', 'head')
The draws below stay inside these ranges and needn't reach their ends.
Inputs may be any that keep to these rules, and one draw needn't show every extreme that they name: Tile g lies at (g // 16, g // 4 % 4, g % 4) in a grid of 4 x 4 x 4 tiles. Entry k of window[g] is either -1 or the tile that lies (k // 9 - 1, k // 3 % 3 - 1, k % 3 - 1) steps away from g along time, height and width; it is -1 where that tile is outside the grid. Entry 13 is g itself.
All inputs are finite; a program needn't handle non-finite values.
Results may differ from the reference program's by a relative error of at most 0.0075.
Values may be sent and summed in bfloat16 or wider, within the bound.
A program may use at most 64 MiB of HBM per device.

```python
import jax
import jax.numpy as jnp
from jax import lax

TILE = 256
HEADS = 24
HEAD_DIM = 128
D = 6144
GH = 4
GW = 4
SLOTS = 27
TILES = 64
GT = 4
TOKENS = 16384


def base_draw(key, stream_id):
    return jnp.clip(jax.random.normal(jax.random.fold_in(key, stream_id), (TOKENS, HEADS * HEAD_DIM)) * 1.5, -6.0, 6.0)


def draw_queries(key, part):
    drawn = base_draw(key, 11)
    return drawn.astype(jnp.bfloat16)


def draw_keys(key, part):
    drawn = base_draw(key, 21)
    return drawn.astype(jnp.bfloat16)


def draw_window(key, part):
    tile_ids = jnp.arange(TILES, dtype=jnp.int32)[:, None]
    slot_ids = jnp.arange(SLOTS, dtype=jnp.int32)[None, :]
    time_pos = tile_ids // (GH * GW)
    row_pos = tile_ids // GW % GH
    col_pos = tile_ids % GW
    time_step = slot_ids // 9 - 1
    row_step = slot_ids // 3 % 3 - 1
    col_step = slot_ids % 3 - 1
    new_time = time_pos + time_step
    new_row = row_pos + row_step
    new_col = col_pos + col_step
    inside = (new_time >= 0) & (new_time < GT) & (new_row >= 0) & (new_row < GH) & (new_col >= 0) & (new_col < GW)
    target = (new_time * GH + new_row) * GW + new_col
    percent = jax.random.randint(jax.random.fold_in(key, 31), (TILES, 1), 30, 101)
    rolled = jax.random.randint(jax.random.fold_in(key, 32), (TILES, SLOTS), 0, 100)
    kept = inside & ((rolled < percent) | (slot_ids == 13))
    return jnp.where(kept, target, -1).astype(jnp.int32)


def steps_of(own_key, dims, cuts, low, largest):
    def one(dim, blocks):
        heights = jax.random.uniform(jax.random.fold_in(jax.random.fold_in(own_key, 6), dim), (blocks,), jnp.float32, low / len(cuts), largest / len(cuts))
        return jnp.repeat(jnp.exp(heights), dims[dim] // blocks).reshape((-1,) + (1,) * (len(dims) - dim - 1))

    factor_of = one(*cuts[0])
    for cut in cuts[1:]:
        factor_of = factor_of * one(*cut)
    return factor_of


def bell_draw(own_key, dims, scale, reach, split=(), held_as=jnp.bfloat16):
    values = scale * jax.random.normal(own_key, dims, jnp.float32)
    if split:
        values = values * steps_of(own_key, dims, split, -0.22, 0.18)
    return jnp.clip(values, -reach, reach).astype(held_as)


def setup_inputs(seed: int = 0) -> dict:
    arg_keys = jax.random.split(jax.random.key(seed), 6)
    queries = draw_queries(jax.random.fold_in(arg_keys[5], 71), 0)
    keys = draw_keys(jax.random.fold_in(arg_keys[5], 71), 0)
    values = bell_draw(arg_keys[2], (TOKENS, HEADS * HEAD_DIM), 1.0, 6.0, ((0, 64), (1, 8)))
    window = draw_window(jax.random.fold_in(arg_keys[5], 71), 0)
    out_weight = bell_draw(arg_keys[4], (HEADS * HEAD_DIM, D), (HEADS * HEAD_DIM) ** -0.5, 0.109375, ((0, 64), (1, 8)))
    return dict(queries=queries, keys=keys, values=values, window=window, out_weight=out_weight)


def reference(queries, keys, values, window, out_weight):
    tile_count = TOKENS // TILE
    tiled = (tile_count, TILE, HEADS, HEAD_DIM)
    query_tiles = queries.reshape(tiled)
    key_tiles = keys.reshape(tiled)
    value_tiles = values.reshape(tiled)
    factor = HEAD_DIM ** -0.5

    def one_tile(tile_item):
        query_block, listed = tile_item
        listed_ok = listed >= 0
        clamped = jnp.where(listed_ok, listed, 0).astype(jnp.int32)
        key_block = key_tiles[clamped].reshape(SLOTS * TILE, HEADS, HEAD_DIM).astype(jnp.float32)
        value_block = value_tiles[clamped].reshape(SLOTS * TILE, HEADS, HEAD_DIM).astype(jnp.float32)
        scores = jnp.einsum("qhd,khd->qhk", query_block.astype(jnp.float32), key_block) * factor
        key_ok = jnp.repeat(listed_ok, TILE)[None, None, :]
        scores = jnp.where(key_ok, scores, -jnp.inf)
        row_max = jnp.max(scores, axis=-1, keepdims=True)
        weights = jnp.exp(scores - row_max)
        denominator = jnp.sum(weights, axis=-1)
        rounded = lax.optimization_barrier(weights.astype(jnp.bfloat16)).astype(jnp.float32)
        numerator = jnp.einsum("qhk,khd->qhd", rounded, value_block)
        return (numerator / denominator[:, :, None]).astype(jnp.bfloat16)

    attended = lax.map(one_tile, (query_tiles, window))
    attended = attended.reshape(TOKENS, HEADS * HEAD_DIM)
    return jnp.dot(attended, out_weight, preferred_element_type=jnp.float32).astype(jnp.bfloat16)
```

```python
import functools

import jax
import jax.numpy as jnp
from jax import lax
from jax.experimental import pallas as pl
from jax.experimental.pallas import tpu as pltpu
from jax.sharding import PartitionSpec as P

MESH = pl.DeviceIdType.MESH
TILE = 256
HD = 128
HEADS_DEV = 3
WIDTH = HD * HEADS_DEV
GROUPS = 8
NEG = -1e30
BIG = 1e30
SCALE = 1.4426950408889634 * HD**-0.5
N_CH = 160


def kernel(q_in, k_in, v_in, bias_in, w_in, out_ref,
           kb, vb, wb, qb, bb, ab, sb, po, ps, ro, rs, lo, ls, send_sem, recv_sem, loc_sem):
    s = lax.axis_index("seq")
    g = lax.axis_index("head")
    y = s // 32
    x = (s // 8) % 4
    z = s % 8
    t = 2 * y + x // 2
    h = 2 * (x % 2) + z // 4
    w = z % 4
    core = g % 2

    def at(yy, xx, zz):
        return (yy * 32 + xx * 8 + zz, g)

    def at_time(tt):
        return (16 * tt + s % 16, g)

    z_up, z_dn = at(y, x, (z + 1) % 8), at(y, x, (z + 7) % 8)
    x_up, x_dn = at(y, (x + 1) % 4, z), at(y, (x + 3) % 4, z)
    x_flip = at(y, x + 1 - 2 * (x % 2), z)
    y_flip = at(1 - y, x, z)
    t_up, t_dn = at_time((t + 1) % 4), at_time((t + 3) % 4)
    partner = (s, g + 1 - 2 * core)

    def peer(d):
        return (s, (g + d) % GROUPS)

    barrier = pltpu.get_barrier_semaphore()
    greeted = [z_up, z_dn, x_up, x_dn, y_flip, t_up, t_dn] + [peer(d) for d in range(1, GROUPS)]
    for other in greeted:
        pl.semaphore_signal(barrier, inc=1, device_id=other, device_id_type=MESH)

    channels = [0]
    sent = []

    def channel(n=1):
        channels[0] += n
        return channels[0] - n

    def copy(src, dst, ch, dev):
        return pltpu.make_async_remote_copy(
            src_ref=src, dst_ref=dst, send_sem=send_sem.at[ch], recv_sem=recv_sem.at[ch],
            device_id=dev, device_id_type=MESH)

    def send(src, dst, ch, dev, cond=None):
        c = copy(src, dst, ch, dev)
        if cond is None:
            c.start()
        else:
            pl.when(cond)(c.start)
        sent.append((c, cond))

    def arrive(dst, ch, cond=None):
        c = copy(dst, dst, ch, z_up)
        if cond is None:
            c.wait_recv()
        else:
            pl.when(cond)(c.wait_recv)

    base = 8 * (x % 2)
    own = base + z
    row0 = pl.multiple_of(g * 32, 32)
    col0 = pl.multiple_of(g * WIDTH, HD)
    local = [
        pltpu.make_async_copy(k_in, kb.at[own], loc_sem.at[0]),
        pltpu.make_async_copy(v_in, vb.at[own], loc_sem.at[1]),
        pltpu.make_async_copy(w_in, wb.at[x, y, z], loc_sem.at[2]),
        pltpu.make_async_copy(q_in.at[:, pl.ds(col0, WIDTH)], qb.at[0, pl.ds(row0, 32)], loc_sem.at[3]),
        pltpu.make_async_copy(bias_in, bb.at[0], loc_sem.at[4]),
    ]
    for c in local:
        c.start()
    pl.semaphore_wait(barrier, len(greeted))

    q_ch = channel(GROUPS)
    for d in range(1, GROUPS):
        col = pl.multiple_of(((g + d) % GROUPS) * WIDTH, HD)
        send(q_in.at[:, pl.ds(col, WIDTH)], qb.at[0, pl.ds(row0, 32)], q_ch + d, peer(d))
    up_k, up_v, dn_k, dn_v = channel(5), channel(5), channel(5), channel(5)
    send(k_in, kb.at[own], up_k + 1, z_up)
    send(k_in, kb.at[own], dn_k + 1, z_dn)
    send(v_in, vb.at[own], up_v + 1, z_up)
    send(v_in, vb.at[own], dn_v + 1, z_dn)
    w_y = channel()
    send(w_in, wb.at[x, y, z], w_y, y_flip)
    for c in local:
        c.wait()

    later, earlier = t < 3, t > 0
    for d in range(1, GROUPS):
        src_row = pl.multiple_of(((g + GROUPS - d) % GROUPS) * 32, 32)
        arrive(qb.at[0, pl.ds(src_row, 32)], q_ch + d)
    q_up, q_dn, b_up, b_dn = channel(), channel(), channel(), channel()
    send(qb.at[0], qb.at[1], q_up, t_up, later)
    send(bb.at[0], bb.at[1], b_up, t_up, later)
    send(qb.at[0], qb.at[2], q_dn, t_dn, earlier)
    send(bb.at[0], bb.at[2], b_dn, t_dn, earlier)

    w_up, w_dn, wx_up, wx_dn = channel(5), channel(5), channel(), channel()

    def weight_to_x(zz):
        send(wb.at[x, :, zz], wb.at[x, :, zz], wx_up, x_up)
        send(wb.at[x, :, zz], wb.at[x, :, zz], wx_dn, x_dn)

    arrive(wb.at[x, 1 - y, z], w_y)
    wx_send = []

    def weight_x(zz, n):
        cu = copy(wb.at[x, :, zz], wb.at[x, :, zz], wx_up, x_up)
        cd = copy(wb.at[x, :, zz], wb.at[x, :, zz], wx_dn, x_dn)
        cu.start()
        cd.start()

    send(wb.at[x, :, z], wb.at[x, :, z], w_up + 1, z_up)
    send(wb.at[x, :, z], wb.at[x, :, z], w_dn + 1, z_dn)
    weight_x(z, 0)

    crossing = z // 4 == x % 2
    e_ch = channel(6)
    for i in range(1, 4):
        below, above = base + (z + 8 - i) % 8, base + (z + i) % 8
        zb, za = (z + 8 - i) % 8, (z + i) % 8
        arrive(kb.at[below], up_k + i)
        send(kb.at[below], kb.at[below], up_k + i + 1, z_up)
        if i == 3:
            up_edge = jnp.logical_and(crossing, w < 3)
            send(kb.at[below], kb.at[below], e_ch + 0, x_flip, up_edge)
        arrive(kb.at[above], dn_k + i)
        if i < 3:
            send(kb.at[above], kb.at[above], dn_k + i + 1, z_dn)
        else:
            dn_edge = jnp.logical_and(crossing, w > 0)
            send(kb.at[above], kb.at[above], e_ch + 2, x_flip, dn_edge)
        arrive(vb.at[below], up_v + i)
        if i < 3:
            send(vb.at[below], vb.at[below], up_v + i + 1, z_up)
        else:
            send(vb.at[below], vb.at[below], e_ch + 1, x_flip, up_edge)
        arrive(vb.at[above], dn_v + i)
        send(vb.at[above], vb.at[above], dn_v + i + 1, z_dn)
        if i == 3:
            send(vb.at[above], vb.at[above], e_ch + 3, x_flip, dn_edge)
        arrive(wb.at[x, :, zb], w_up + i)
        if i < 3:
            send(wb.at[x, :, zb], wb.at[x, :, zb], w_up + i + 1, z_up)
        else:
            send(wb.at[x, 0, zb], wb.at[x, 0, zb], w_up + i + 1, z_up)
        arrive(wb.at[x, :, za], w_dn + i)
        if i < 3:
            send(wb.at[x, :, za], wb.at[x, :, za], w_dn + i + 1, z_dn)
        else:
            send(wb.at[x, 1, za], wb.at[x, 1, za], w_dn + i + 1, z_dn)
        weight_x(zb, i)
        weight_x(za, i)
    zf = (z + 4) % 8
    far = base + zf
    arrive(kb.at[far], up_k + 4)
    send(kb.at[far], kb.at[far], e_ch + 4, x_flip, crossing)
    arrive(vb.at[far], dn_v + 4)
    send(vb.at[far], vb.at[far], e_ch + 5, x_flip, crossing)
    arrive(wb.at[x, 0, zf], w_up + 4)
    arrive(wb.at[x, 1, zf], w_dn + 4)
    weight_x(zf, 4)

    arrive(qb.at[1], q_up, earlier)
    arrive(bb.at[1], b_up, earlier)
    arrive(qb.at[2], q_dn, later)
    arrive(bb.at[2], b_dn, later)

    facing = z // 4 != x % 2
    over = 8 - base + z
    fz = 8 - base + (z + 4) % 8
    up_face = jnp.logical_and(facing, w < 3)
    dn_face = jnp.logical_and(facing, w > 0)
    f_up = 8 - base + (z + 5) % 8
    f_dn = 8 - base + (z + 3) % 8
    arrive(kb.at[f_up], e_ch + 0, up_face)
    arrive(vb.at[f_up], e_ch + 1, up_face)
    arrive(kb.at[f_dn], e_ch + 2, dn_face)
    arrive(vb.at[f_dn], e_ch + 3, dn_face)
    arrive(kb.at[fz], e_ch + 4, facing)
    arrive(vb.at[fz], e_ch + 5, facing)

    h_at = [h - (h + 3) // 4, h, h + 1 - h // 3]
    w_at = [w - (w + 3) // 4, w, w + 1 - w // 3]
    slots = [h_at[n // 3] * 4 + w_at[n % 3] for n in range(9)]
    lane = lax.broadcasted_iota(jnp.int32, (TILE, HD), 1)

    def unit(i, a):
        first = (9, 18, 0)[i]
        cols = pl.ds(pl.multiple_of(a * HD, HD), HD)
        q = qb[i, :, cols]
        m = jnp.full((TILE, HD), NEG, jnp.float32)
        for n in range(9):
            sc = lax.dot_general(q, kb[slots[n], :, cols], (((1,), (1,)), ((), ())),
                                 preferred_element_type=jnp.float32)
            sb[n] = sc
            m = jnp.maximum(m, jnp.maximum(sc[:, :HD], sc[:, HD:]) - bb[i, first + n : first + n + 1, :])
        m = jnp.max(m, axis=1, keepdims=True) * SCALE
        ones = jnp.ones((TILE, HD), jnp.bfloat16)
        acc = jnp.zeros((TILE, 2 * HD), jnp.float32)
        for n in range(9):
            shift = m + bb[i, first + n : first + n + 1, :]
            p = jnp.exp2(sb[n] * SCALE - jnp.concatenate([shift, shift], axis=1))
            v = jnp.concatenate([vb[slots[n], :, cols], ones], axis=1)
            acc = acc + jnp.dot(p.astype(jnp.bfloat16), v, preferred_element_type=jnp.float32)
        return m, acc

    po_ch, ps_ch = channel(6), channel(6)
    a_ch, c_ch = channel(9), channel(12)
    edge = ((1, earlier, t_dn), (2, later, t_up))

    def missing(k, cond):
        @pl.when(cond)
        def _():
            rs[k] = jnp.full((HEADS_DEV, 8, TILE), NEG, jnp.float32)
            ro[k] = jnp.zeros((HEADS_DEV, TILE, HD), jnp.bfloat16)

    missing(0, t == 0)
    missing(1, t == 3)

    def back(k, a, dev):
        return (copy(po.at[k, a], ro.at[1 - k, a], po_ch + 3 * k + a, dev),
                copy(ps.at[k, a], rs.at[1 - k, a], ps_ch + 3 * k + a, dev))

    def feature(gg, a):
        return ab.at[:, pl.ds(pl.multiple_of(gg * WIDTH + a * HD, HD), HD)]

    def remote_units(a):
        for i, cond, dev in edge:
            @pl.when(cond)
            def _(i=i, dev=dev):
                m, acc = unit(i, a)
                k = i - 1
                po[k, a] = acc[:, :HD].astype(jnp.bfloat16)
                stat = jnp.where(lane == 0, m, acc[:, HD:])
                ps[k, a] = stat.T[:8]
                for c in back(k, a, dev):
                    c.start()

    def own_unit(a):
        m, acc = unit(0, a)
        lo[...] = acc
        ls[...] = jnp.broadcast_to(m, (TILE, HD))

    def share(gg, a, ch, dev):
        return copy(feature(gg, a), feature(gg, a), ch, dev)

    def finish(a):
        for k, cond in ((0, earlier), (1, later)):
            @pl.when(cond)
            def _(k=k):
                copy(ro.at[k, a], ro.at[k, a], po_ch + 3 * (1 - k) + a, t_up).wait_recv()
                copy(rs.at[k, a], rs.at[k, a], ps_ch + 3 * (1 - k) + a, t_up).wait_recv()
        m0, num0, den0 = ls[...][:, :1], lo[:, :HD], lo[:, HD:]
        stats = []
        for k in range(2):
            r = rs[k, a]
            st = jnp.concatenate([r] * 16, axis=0).T
            stats.append((st[:, :1], st[:, 1:2]))
        top = jnp.maximum(m0, jnp.maximum(stats[0][0], stats[1][0]))
        f0 = jnp.exp2(m0 - top)
        num, den = num0 * f0, den0 * f0
        for k in range(2):
            mk, lk = stats[k]
            f = jnp.exp2(mk - top)
            num = num + ro[k, a].astype(jnp.float32) * f
            den = den + jnp.maximum(lk, 0.0) * f
        feature(g, a)[...] = (num / den).astype(jnp.bfloat16)
        for d in range(1, 4):
            share(g, a, a_ch + 3 * (d - 1) + a, peer(2 * d)).start()
        share(g, a, c_ch + a, partner).start()

    def head_step(a, _):
        remote_units(a)

        @pl.when(a > 0)
        def _():
            finish(a - 1)

        own_unit(a)
        return 0

    lax.fori_loop(0, 1, head_step, 0)
    xl, xr = (x + 3) % 4, (x + 1) % 4
    xf = (x + 2) % 4
    w2_up, w2_dn = channel(), channel()
    arrive(wb.at[xl], wx_up)
    send(wb.at[xl, 0], wb.at[xl, 0], w2_up, x_up)
    arrive(wb.at[xr], wx_dn)
    send(wb.at[xr, 1], wb.at[xr, 1], w2_dn, x_dn)
    lax.fori_loop(1, HEADS_DEV, head_step, 0)
    finish(HEADS_DEV - 1)

    for a in range(HEADS_DEV):
        for d in range(1, 4):
            src = (g + GROUPS - 2 * d) % GROUPS
            copy(feature(src, a), feature(src, a), a_ch + 3 * (d - 1) + a, z_up).wait_recv()
            share(src, a, c_ch + 3 * d + a, partner).start()
    arrive(wb.at[xf, 0], w2_up)
    arrive(wb.at[xf, 1], w2_dn)
    for a in range(HEADS_DEV):
        for d in range(4):
            src = (g + 1 - 2 * core + GROUPS - 2 * d) % GROUPS
            copy(feature(src, a), feature(src, a), c_ch + 3 * d + a, z_up).wait_recv()

    for n in range(3):
        cols = slice(n * 256, n * 256 + 256)
        acc = jnp.zeros((TILE, 256), jnp.float32)
        for j in range(GROUPS):
            rows = wb[j % 4, j // 4, :, :, cols].reshape(WIDTH, 256)
            acc = acc + jnp.dot(ab[:, j * WIDTH : (j + 1) * WIDTH], rows, preferred_element_type=jnp.float32)
        out_ref[:, cols] = acc.astype(jnp.bfloat16)

    for c, cond in sent:
        if cond is None:
            c.wait_send()
        else:
            pl.when(cond)(c.wait_send)
    copy(wb.at[x], wb.at[x], wx_up, x_up).wait_send()
    copy(wb.at[x], wb.at[x], wx_dn, x_dn).wait_send()
    for a in range(HEADS_DEV):
        for i, cond, dev in edge:
            for c in back(i - 1, a, dev):
                pl.when(cond)(c.wait_send)
        for d in range(1, 4):
            share(g, a, a_ch + 3 * (d - 1) + a, peer(2 * d)).wait_send()
        for d in range(4):
            share(g, a, c_ch + 3 * d + a, partner).wait_send()
    assert channels[0] <= N_CH


def local(queries, keys, values, window, out_weight):
    listed = jnp.where(window[0] >= 0, 0.0, BIG).astype(jnp.float32)
    bias = jnp.broadcast_to(jnp.pad(listed, (0, 5))[:, None], (32, HD))
    any_spec = pl.BlockSpec(memory_space=pl.ANY)
    bf16, f32 = jnp.bfloat16, jnp.float32
    return pl.pallas_call(
        kernel,
        out_shape=jax.ShapeDtypeStruct((TILE, out_weight.shape[1]), bf16),
        in_specs=[any_spec] * 5,
        out_specs=pl.BlockSpec(memory_space=pltpu.VMEM),
        scratch_shapes=[
            pltpu.VMEM((16, TILE, WIDTH), bf16),
            pltpu.VMEM((16, TILE, WIDTH), bf16),
            pltpu.VMEM((4, 2, 8, 48, 768), bf16),
            pltpu.VMEM((3, TILE, WIDTH), bf16),
            pltpu.VMEM((3, 32, HD), f32),
            pltpu.VMEM((TILE, GROUPS * WIDTH), bf16),
            pltpu.VMEM((9, TILE, TILE), f32),
            pltpu.VMEM((2, HEADS_DEV, TILE, HD), bf16),
            pltpu.VMEM((2, HEADS_DEV, 8, TILE), f32),
            pltpu.VMEM((2, HEADS_DEV, TILE, HD), bf16),
            pltpu.VMEM((2, HEADS_DEV, 8, TILE), f32),
            pltpu.VMEM((TILE, 2 * HD), f32),
            pltpu.VMEM((TILE, HD), f32),
            pltpu.SemaphoreType.DMA((N_CH,)),
            pltpu.SemaphoreType.DMA((N_CH,)),
            pltpu.SemaphoreType.DMA((5,)),
        ],
        compiler_params=pltpu.CompilerParams(
            collective_id=0, has_side_effects=True, vmem_limit_bytes=60 * 1024 * 1024),
    )(queries, keys, values, bias, out_weight)


def solution(mesh):
    in_specs = (
        P(("seq", "head"), None),
        P("seq", "head"),
        P("seq", "head"),
        P("seq", None),
        P("seq", "head"),
    )
    return jax.shard_map(local, mesh=mesh, in_specs=in_specs, out_specs=P("seq", "head"), check_vma=False)
```

```python
import functools

import jax
import jax.numpy as jnp
from jax import lax
from jax.experimental import pallas as pl
from jax.experimental.pallas import tpu as pltpu
from jax.sharding import PartitionSpec as P

MESH = pl.DeviceIdType.MESH
TILE = 256
HD = 128
HEADS_DEV = 3
WIDTH = HD * HEADS_DEV
GROUPS = 8
NEG = -1e30
BIG = 1e30
SCALE = 1.4426950408889634 * HD**-0.5
N_CH = 200


def kernel(q_in, k_in, v_in, win, w_in, out_ref,
           kv, wb, qb, bb, ab, sb, po, ps, ro, rs, lo, ls, send_sem, recv_sem, loc_sem):
    s = lax.axis_index("seq")
    g = lax.axis_index("head")
    y = s // 32
    x = (s // 8) % 4
    z = s % 8
    t = 2 * y + x // 2
    h = 2 * (x % 2) + z // 4
    w = z % 4
    core = g % 2

    def at(yy, xx, zz):
        return (yy * 32 + xx * 8 + zz, g)

    def at_time(tt):
        return (16 * tt + s % 16, g)

    z_up, z_dn = at(y, x, (z + 1) % 8), at(y, x, (z + 7) % 8)
    x_up, x_dn = at(y, (x + 1) % 4, z), at(y, (x + 3) % 4, z)
    x_flip = at(y, x + 1 - 2 * (x % 2), z)
    y_flip = at(1 - y, x, z)
    t_up, t_dn = at_time((t + 1) % 4), at_time((t + 3) % 4)
    partner = (s, g + 1 - 2 * core)

    def peer(d):
        return (s, (g + d) % GROUPS)

    barrier = pltpu.get_barrier_semaphore()
    greeted = [z_up, z_dn, x_up, x_dn, y_flip, t_up, t_dn] + [peer(d) for d in range(1, GROUPS)]
    for other in greeted:
        pl.semaphore_signal(barrier, inc=1, device_id=other, device_id_type=MESH)

    channels = [0]
    draining = [False]
    done = {}

    def channel(n=1):
        channels[0] += n
        return channels[0] - n

    def copy(src, dst, ch, dev):
        return pltpu.make_async_remote_copy(
            src_ref=src, dst_ref=dst, send_sem=send_sem.at[ch], recv_sem=recv_sem.at[ch],
            device_id=dev, device_id_type=MESH)

    def send(ref, ch, dev, cond=None, dst=None):
        c = copy(ref, ref if dst is None else dst, ch, dev)
        act = c.wait_send if draining[0] else c.start
        if cond is None:
            act()
        else:
            pl.when(cond)(act)

    def do(step, *which):
        step(*which)
        done[step, which] = None

    def arrive(dst, ch, cond=None):
        if draining[0]:
            return
        c = copy(dst, dst, ch, z_up)
        if cond is None:
            c.wait_recv()
        else:
            pl.when(cond)(c.wait_recv)

    base = 8 * (x % 2)
    own = base + z
    row0 = pl.multiple_of(g * 32, 32)
    col0 = pl.multiple_of(g * WIDTH, HD)
    local = []
    for a in range(HEADS_DEV):
        cols = pl.ds(a * HD, HD)
        local.append(pltpu.make_async_copy(k_in.at[:, cols], kv.at[own, a, 0], loc_sem.at[2 * a]))
        local.append(pltpu.make_async_copy(v_in.at[:, cols], kv.at[own, a, 1], loc_sem.at[2 * a + 1]))
    for p in range(2):
        local.append(pltpu.make_async_copy(w_in.at[:, pl.ds(p * WIDTH, WIDTH)], wb.at[p, x, y, z], loc_sem.at[6 + p]))
    local.append(pltpu.make_async_copy(q_in.at[:, pl.ds(col0, WIDTH)], qb.at[0, pl.ds(row0, 32)], loc_sem.at[8]))
    for c in local:
        c.start()
    for n in range(27):
        bb[0, n : n + 1, :] = jnp.full((1, HD), jnp.where(win[0, n] >= 0, 0.0, BIG), jnp.float32)
    for c in local:
        c.wait()
    pl.semaphore_wait(barrier, len(greeted))

    up, dn = channel(15), channel(15)
    e_ch = channel(9)
    q_ch = channel(GROUPS)
    w_y = channel()
    w_up, w_dn = channel(10), channel(10)
    x_up_ch, x_dn_ch, x2_ch = channel(16), channel(16), channel(16)
    wy_ch = channel(4)
    later, earlier = t < 3, t > 0

    def own_block(a):
        send(kv.at[own, a], up + 3 + a, z_up)
        send(kv.at[own, a], dn + 3 + a, z_dn)

    crossing = z // 4 == x % 2
    up_edge = jnp.logical_and(crossing, w < 3)
    dn_edge = jnp.logical_and(crossing, w > 0)

    def ring(i, a):
        below, above = base + (z + 8 - i) % 8, base + (z + i) % 8
        if i == 4:
            arrive(kv.at[below, a, 0], up + 3 * i + a)
            arrive(kv.at[below, a, 1], dn + 3 * i + a)
            send(kv.at[below, a], e_ch + a, x_flip, crossing)
            return
        arrive(kv.at[below, a], up + 3 * i + a)
        if i < 3:
            send(kv.at[below, a], up + 3 * i + 3 + a, z_up)
        else:
            send(kv.at[below, a, 0], up + 3 * i + 3 + a, z_up)
            send(kv.at[below, a], e_ch + 3 + a, x_flip, up_edge)
        arrive(kv.at[above, a], dn + 3 * i + a)
        if i < 3:
            send(kv.at[above, a], dn + 3 * i + 3 + a, z_dn)
        else:
            send(kv.at[above, a, 1], dn + 3 * i + 3 + a, z_dn)
            send(kv.at[above, a], e_ch + 6 + a, x_flip, dn_edge)

    def z_of(n):
        return (z + 8 - (n + 1) // 2) % 8 if n % 2 else (z + n // 2) % 8

    def part(p, xx, zz):
        return wb.at[0, xx, :, zz] if p == 0 else wb.at[1, xx, y, zz]

    def weight_x(n):
        for p in range(2):
            send(part(p, x, z_of(n)), x_up_ch + 2 * n + p, x_up)
            send(part(p, x, z_of(n)), x_dn_ch + 2 * n + p, x_dn)

    def weight_z(i):
        zb, za = (z + 8 - i) % 8, (z + i) % 8
        for p in range(2):
            if i == 0:
                send(part(p, x, z), w_up + p, z_up)
                send(part(p, x, z), w_dn + p, z_dn)
                continue
            if i == 4:
                continue
            arrive(part(p, x, zb), w_up + 2 * i - 2 + p)
            arrive(part(p, x, za), w_dn + 2 * i - 2 + p)
            if i < 3:
                send(part(p, x, zb), w_up + 2 * i + p, z_up)
                send(part(p, x, za), w_dn + 2 * i + p, z_dn)
            elif p == 0:
                send(wb.at[0, x, 0, zb], w_up + 6, z_up)
                send(wb.at[0, x, 1, za], w_dn + 6, z_dn)
            else:
                send(part(1, x, zb), w_up + 7, z_up)
        if i == 0:
            weight_x(0)
        elif i < 4:
            weight_x(2 * i - 1)
            weight_x(2 * i)
        else:
            arrive(wb.at[0, x, 0, zb], w_up + 6)
            arrive(wb.at[0, x, 1, za], w_dn + 6)
            arrive(part(1, x, zb), w_up + 7)
            weight_x(7)

    xl, xr, xf = (x + 3) % 4, (x + 1) % 4, (x + 2) % 4
    low = z < 4

    def weight_x2(n):
        for p in range(2):
            arrive(part(p, xl, z_of(n)), x_up_ch + 2 * n + p)
            arrive(part(p, xr, z_of(n)), x_dn_ch + 2 * n + p)
            send(part(p, xl, z_of(n)), x2_ch + 2 * n + p, x_up, z >= 4)
            send(part(p, xr, z_of(n)), x2_ch + 2 * n + p, x_dn, low)

    def weight_y():
        for n, xx in enumerate((x, xl, xr)):
            send(wb.at[1, xx, y], wy_ch + n, y_flip)

    def weight_y2():
        for n in range(8):
            for p in range(2):
                arrive(part(p, xf, z_of(n)), x2_ch + 2 * n + p)
        send(wb.at[1, xf, y], wy_ch + 3, y_flip)

    qt = channel(4)

    def query_out():
        for d in range(1, GROUPS):
            col = pl.multiple_of(((g + d) % GROUPS) * WIDTH, HD)
            send(q_in.at[:, pl.ds(col, WIDTH)], q_ch + d, peer(d), dst=qb.at[0, pl.ds(row0, 32)])

    def query_time():
        for d in range(1, GROUPS):
            src_row = pl.multiple_of(((g + GROUPS - d) % GROUPS) * 32, 32)
            arrive(qb.at[0, pl.ds(src_row, 32)], q_ch + d)
        send(qb.at[0], qt, t_up, later, dst=qb.at[1])
        send(bb.at[0], qt + 1, t_up, later, dst=bb.at[1])
        send(qb.at[0], qt + 2, t_dn, earlier, dst=qb.at[2])
        send(bb.at[0], qt + 3, t_dn, earlier, dst=bb.at[2])

    def weight_pair():
        send(wb.at[0, x, y, z], w_y, y_flip)

    do(own_block, 0)
    do(query_out)
    do(weight_pair)
    do(own_block, 1)
    do(ring, 1, 0)
    arrive(wb.at[0, x, 1 - y, z], w_y)
    do(weight_z, 0)
    do(own_block, 2)
    do(ring, 2, 0)
    do(query_time)
    do(ring, 1, 1)
    do(weight_z, 1)
    do(ring, 3, 0)
    do(ring, 2, 1)
    do(weight_z, 2)
    do(ring, 4, 0)
    do(ring, 1, 2)
    do(weight_z, 3)
    do(ring, 3, 1)
    do(ring, 2, 2)
    do(weight_x2, 0)
    do(weight_x2, 1)
    do(weight_x2, 2)
    do(weight_z, 4)
    do(ring, 4, 1)

    h_at = [h - (h + 3) // 4, h, h + 1 - h // 3]
    w_at = [w - (w + 3) // 4, w, w + 1 - w // 3]
    slots = [h_at[n // 3] * 4 + w_at[n % 3] for n in range(9)]
    lane = lax.broadcasted_iota(jnp.int32, (TILE, HD), 1)

    def unit(i, a):
        first = (9, 18, 0)[i]
        q = qb[i, :, pl.ds(pl.multiple_of(a * HD, HD), HD)]
        m = jnp.full((TILE, HD), NEG, jnp.float32)
        for n in range(9):
            sc = lax.dot_general(q, kv[slots[n], a, 0], (((1,), (1,)), ((), ())),
                                 preferred_element_type=jnp.float32)
            sb[n] = sc
            m = jnp.maximum(m, jnp.maximum(sc[:, :HD], sc[:, HD:]) - bb[i, first + n : first + n + 1, :])
        m = jnp.max(m, axis=1, keepdims=True) * SCALE
        ones = jnp.ones((TILE, HD), jnp.bfloat16)
        acc = jnp.zeros((TILE, 2 * HD), jnp.float32)
        for n in range(9):
            shift = m + bb[i, first + n : first + n + 1, :]
            p = jnp.exp2(sb[n] * SCALE - jnp.concatenate([shift, shift], axis=1))
            v = jnp.concatenate([kv[slots[n], a, 1], ones], axis=1)
            acc = acc + jnp.dot(p.astype(jnp.bfloat16), v, preferred_element_type=jnp.float32)
        return m, acc

    po_ch, ps_ch = channel(6), channel(6)
    a_ch, c_ch = channel(9), channel(12)
    edge = ((1, earlier, t_dn), (2, later, t_up))

    def missing(k, cond):
        @pl.when(cond)
        def _():
            rs[k] = jnp.full((HEADS_DEV, 8, TILE), NEG, jnp.float32)
            ro[k] = jnp.zeros((HEADS_DEV, TILE, HD), jnp.bfloat16)

    missing(0, t == 0)
    missing(1, t == 3)

    def back(k, a, dev):
        return (copy(po.at[k, a], ro.at[1 - k, a], po_ch + 3 * k + a, dev),
                copy(ps.at[k, a], rs.at[1 - k, a], ps_ch + 3 * k + a, dev))

    def feature(gg, a):
        return ab.at[:, pl.ds(pl.multiple_of(gg * WIDTH + a * HD, HD), HD)]

    def remote_unit(j, a):
        i, cond, dev = edge[j]

        @pl.when(cond)
        def _():
            m, acc = unit(i, a)
            k = i - 1
            po[k, a] = acc[:, :HD].astype(jnp.bfloat16)
            stat = jnp.where(lane == 0, m, acc[:, HD:])
            ps[k, a] = stat.T[:8]
            for c in back(k, a, dev):
                c.start()

    def own_unit(a):
        m, acc = unit(0, a)
        lo[a % 2] = acc
        ls[a % 2] = jnp.broadcast_to(m, (TILE, HD))

    def share(gg, a, ch, dev):
        return copy(feature(gg, a), feature(gg, a), ch, dev)

    def finish(a):
        for k, cond in ((0, earlier), (1, later)):
            @pl.when(cond)
            def _(k=k):
                copy(ro.at[k, a], ro.at[k, a], po_ch + 3 * (1 - k) + a, t_up).wait_recv()
                copy(rs.at[k, a], rs.at[k, a], ps_ch + 3 * (1 - k) + a, t_up).wait_recv()
        m0, num0, den0 = ls[a % 2][:, :1], lo[a % 2, :, :HD], lo[a % 2, :, HD:]
        stats = []
        for k in range(2):
            r = rs[k, a]
            st = jnp.concatenate([r] * 16, axis=0).T
            stats.append((st[:, :1], st[:, 1:2]))
        top = jnp.maximum(m0, jnp.maximum(stats[0][0], stats[1][0]))
        f0 = jnp.exp2(m0 - top)
        num, den = num0 * f0, den0 * f0
        for k in range(2):
            mk, lk = stats[k]
            f = jnp.exp2(mk - top)
            num = num + ro[k, a].astype(jnp.float32) * f
            den = den + jnp.maximum(lk, 0.0) * f
        feature(g, a)[...] = (num / den).astype(jnp.bfloat16)
        for d in range(1, 4):
            share(g, a, a_ch + 3 * (d - 1) + a, peer(2 * d)).start()
        share(g, a, c_ch + a, partner).start()

    def relay(a):
        for d in range(1, 4):
            src = (g + GROUPS - 2 * d) % GROUPS
            copy(feature(src, a), feature(src, a), a_ch + 3 * (d - 1) + a, z_up).wait_recv()
            share(src, a, c_ch + 3 * d + a, partner).start()

    arrive(qb.at[1], qt, earlier)
    arrive(bb.at[1], qt + 1, earlier)
    arrive(qb.at[2], qt + 2, later)
    arrive(bb.at[2], qt + 3, later)

    facing = z // 4 != x % 2
    up_face = jnp.logical_and(facing, w < 3)
    dn_face = jnp.logical_and(facing, w > 0)

    def crossed(a):
        arrive(kv.at[8 - base + (z + 5) % 8, a], e_ch + 3 + a, up_face)
        arrive(kv.at[8 - base + (z + 3) % 8, a], e_ch + 6 + a, dn_face)
        arrive(kv.at[8 - base + (z + 4) % 8, a], e_ch + a, facing)

    def head_step(a, _):
        crossed(a)
        remote_unit(0, a)

        @pl.when(a == 0)
        def _():
            do(ring, 3, 2)

        remote_unit(1, a)

        @pl.when(a == 0)
        def _():
            do(ring, 4, 2)

        @pl.when(a > 0)
        def _():
            finish(a - 1)

        @pl.when(a == 1)
        def _():
            for n in range(3, 8):
                do(weight_x2, n)
            do(weight_y)

        own_unit(a)

        @pl.when(a == 2)
        def _():
            relay(0)
            do(weight_y2)

        return 0

    lax.fori_loop(0, HEADS_DEV, head_step, 0)
    finish(HEADS_DEV - 1)
    relay(1)
    for n, xx in enumerate((x, xl, xr, xf)):
        arrive(wb.at[1, xx, 1 - y], wy_ch + n)
    relay(2)
    for a in range(HEADS_DEV):
        for d in range(4):
            src = (g + 1 - 2 * core + GROUPS - 2 * d) % GROUPS
            copy(feature(src, a), feature(src, a), c_ch + 3 * d + a, z_up).wait_recv()

    for n in range(3):
        acc = jnp.zeros((TILE, 256), jnp.float32)
        for j in range(GROUPS):
            if n == 1:
                rows = jnp.concatenate([wb[0, j % 4, j // 4, :, :, 256:], wb[1, j % 4, j // 4, :, :, :128]], axis=2)
            else:
                rows = wb[n // 2, j % 4, j // 4, :, :, (0, 0, 128)[n] : (256, 0, 384)[n]]
            acc = acc + jnp.dot(ab[:, j * WIDTH : (j + 1) * WIDTH], rows.reshape(WIDTH, 256),
                                preferred_element_type=jnp.float32)
        out_ref[:, n * 256 : n * 256 + 256] = acc.astype(jnp.bfloat16)

    draining[0] = True
    for step, which in done:
        step(*which)
    for a in range(HEADS_DEV):
        for i, cond, dev in edge:
            for c in back(i - 1, a, dev):
                pl.when(cond)(c.wait_send)
        for d in range(1, 4):
            share(g, a, a_ch + 3 * (d - 1) + a, peer(2 * d)).wait_send()
        for d in range(4):
            share(g, a, c_ch + 3 * d + a, partner).wait_send()
    assert channels[0] <= N_CH


def local(queries, keys, values, window, out_weight):
    any_spec = pl.BlockSpec(memory_space=pl.ANY)
    bf16, f32 = jnp.bfloat16, jnp.float32
    return pl.pallas_call(
        kernel,
        out_shape=jax.ShapeDtypeStruct((TILE, out_weight.shape[1]), bf16),
        in_specs=[any_spec] * 3 + [pl.BlockSpec(memory_space=pltpu.SMEM), any_spec],
        out_specs=pl.BlockSpec(memory_space=pltpu.VMEM),
        scratch_shapes=[
            pltpu.VMEM((16, HEADS_DEV, 2, TILE, HD), bf16),
            pltpu.VMEM((2, 4, 2, 8, 48, WIDTH), bf16),
            pltpu.VMEM((3, TILE, WIDTH), bf16),
            pltpu.VMEM((3, 32, HD), f32),
            pltpu.VMEM((TILE, GROUPS * WIDTH), bf16),
            pltpu.VMEM((9, TILE, TILE), f32),
            pltpu.VMEM((2, HEADS_DEV, TILE, HD), bf16),
            pltpu.VMEM((2, HEADS_DEV, 8, TILE), f32),
            pltpu.VMEM((2, HEADS_DEV, TILE, HD), bf16),
            pltpu.VMEM((2, HEADS_DEV, 8, TILE), f32),
            pltpu.VMEM((2, TILE, 2 * HD), f32),
            pltpu.VMEM((2, TILE, HD), f32),
            pltpu.SemaphoreType.DMA((N_CH,)),
            pltpu.SemaphoreType.DMA((N_CH,)),
            pltpu.SemaphoreType.DMA((9,)),
        ],
        compiler_params=pltpu.CompilerParams(
            collective_id=0, has_side_effects=True, vmem_limit_bytes=60 * 1024 * 1024),
    )(queries, keys, values, window, out_weight)


def solution(mesh):
    in_specs = (
        P(("seq", "head"), None),
        P("seq", "head"),
        P("seq", "head"),
        P("seq", None),
        P("seq", "head"),
    )
    return jax.shard_map(local, mesh=mesh, in_specs=in_specs, out_specs=P("seq", "head"), check_vma=False)
```

```python
import functools

import jax
import jax.numpy as jnp
from jax import lax
from jax.experimental import pallas as pl
from jax.experimental.pallas import tpu as pltpu
from jax.sharding import PartitionSpec as P

MESH = pl.DeviceIdType.MESH
TILE = 256
HD = 128
HEADS_DEV = 3
WIDTH = HD * HEADS_DEV
GROUPS = 8
NEG = -1e30
BIG = 1e30
SCALE = 1.4426950408889634 * HD**-0.5
N_CH = 200


def kernel(q_in, k_in, v_in, win, w_in, out_ref,
           kv, wb, qb, bb, ab, sb, po, ps, ro, rs, lo, ls, send_sem, recv_sem, loc_sem):
    s = lax.axis_index("seq")
    g = lax.axis_index("head")
    y = s // 32
    x = (s // 8) % 4
    z = s % 8
    t = 2 * y + x // 2
    h = 2 * (x % 2) + z // 4
    w = z % 4
    core = g % 2

    def at(yy, xx, zz):
        return (yy * 32 + xx * 8 + zz, g)

    def at_time(tt):
        return (16 * tt + s % 16, g)

    z_up, z_dn = at(y, x, (z + 1) % 8), at(y, x, (z + 7) % 8)
    x_up, x_dn = at(y, (x + 1) % 4, z), at(y, (x + 3) % 4, z)
    x_flip = at(y, x + 1 - 2 * (x % 2), z)
    y_flip = at(1 - y, x, z)
    t_up, t_dn = at_time((t + 1) % 4), at_time((t + 3) % 4)
    partner = (s, g + 1 - 2 * core)

    def peer(d):
        return (s, (g + d) % GROUPS)

    barrier = pltpu.get_barrier_semaphore()
    greeted = [z_up, z_dn, x_up, x_dn, y_flip, t_up, t_dn] + [peer(d) for d in range(1, GROUPS)]
    for other in greeted:
        pl.semaphore_signal(barrier, inc=1, device_id=other, device_id_type=MESH)

    channels = [0]
    draining = [False]
    done = {}

    def channel(n=1):
        channels[0] += n
        return channels[0] - n

    def copy(src, dst, ch, dev):
        return pltpu.make_async_remote_copy(
            src_ref=src, dst_ref=dst, send_sem=send_sem.at[ch], recv_sem=recv_sem.at[ch],
            device_id=dev, device_id_type=MESH)

    def send(ref, ch, dev, cond=None, dst=None):
        c = copy(ref, ref if dst is None else dst, ch, dev)
        act = c.wait_send if draining[0] else c.start
        if cond is None:
            act()
        else:
            pl.when(cond)(act)

    def do(step, *which):
        step(*which)
        done[step, which] = None

    def arrive(dst, ch, cond=None):
        if draining[0]:
            return
        c = copy(dst, dst, ch, z_up)
        if cond is None:
            c.wait_recv()
        else:
            pl.when(cond)(c.wait_recv)

    base = 8 * (x % 2)
    own = base + z
    row0 = pl.multiple_of(g * 32, 32)
    col0 = pl.multiple_of(g * WIDTH, HD)
    local = []
    for a in range(HEADS_DEV):
        cols = pl.ds(a * HD, HD)
        local.append(pltpu.make_async_copy(k_in.at[:, cols], kv.at[own, a, 0], loc_sem.at[2 * a]))
        local.append(pltpu.make_async_copy(v_in.at[:, cols], kv.at[own, a, 1], loc_sem.at[2 * a + 1]))
    for p in range(2):
        local.append(pltpu.make_async_copy(w_in.at[:, pl.ds(p * WIDTH, WIDTH)], wb.at[p, x, y, z], loc_sem.at[6 + p]))
    local.append(pltpu.make_async_copy(q_in.at[:, pl.ds(col0, WIDTH)], qb.at[0, pl.ds(row0, 32)], loc_sem.at[8]))
    for c in local:
        c.start()
    for n in range(27):
        bb[0, n : n + 1, :] = jnp.full((1, HD), jnp.where(win[0, n] >= 0, 0.0, BIG), jnp.float32)
    for c in local:
        c.wait()
    pl.semaphore_wait(barrier, len(greeted))

    up, dn = channel(15), channel(15)
    e_ch = channel(9)
    q_ch = channel(GROUPS)
    w_y = channel()
    w_up, w_dn = channel(10), channel(10)
    x_up_ch, x_dn_ch, x2_ch = channel(16), channel(16), channel(16)
    wy_ch = channel(4)
    later, earlier = t < 3, t > 0

    def own_block(a):
        send(kv.at[own, a], up + 3 + a, z_up)
        send(kv.at[own, a], dn + 3 + a, z_dn)

    crossing = z // 4 == x % 2
    up_edge = jnp.logical_and(crossing, w < 3)
    dn_edge = jnp.logical_and(crossing, w > 0)

    def ring(i, a):
        below, above = base + (z + 8 - i) % 8, base + (z + i) % 8
        if i == 4:
            arrive(kv.at[below, a, 0], up + 3 * i + a)
            arrive(kv.at[below, a, 1], dn + 3 * i + a)
            send(kv.at[below, a], e_ch + a, x_flip, crossing)
            return
        arrive(kv.at[below, a], up + 3 * i + a)
        if i < 3:
            send(kv.at[below, a], up + 3 * i + 3 + a, z_up)
        else:
            send(kv.at[below, a, 0], up + 3 * i + 3 + a, z_up)
            send(kv.at[below, a], e_ch + 3 + a, x_flip, up_edge)
        arrive(kv.at[above, a], dn + 3 * i + a)
        if i < 3:
            send(kv.at[above, a], dn + 3 * i + 3 + a, z_dn)
        else:
            send(kv.at[above, a, 1], dn + 3 * i + 3 + a, z_dn)
            send(kv.at[above, a], e_ch + 6 + a, x_flip, dn_edge)

    def z_of(n):
        return (z + 8 - (n + 1) // 2) % 8 if n % 2 else (z + n // 2) % 8

    def part(p, xx, zz):
        return wb.at[0, xx, :, zz] if p == 0 else wb.at[1, xx, y, zz]

    def weight_x(n):
        for p in range(2):
            send(part(p, x, z_of(n)), x_up_ch + 2 * n + p, x_up)
            send(part(p, x, z_of(n)), x_dn_ch + 2 * n + p, x_dn)

    def weight_z(i):
        zb, za = (z + 8 - i) % 8, (z + i) % 8
        for p in range(2):
            if i == 0:
                send(part(p, x, z), w_up + p, z_up)
                send(part(p, x, z), w_dn + p, z_dn)
                continue
            if i == 4:
                continue
            arrive(part(p, x, zb), w_up + 2 * i - 2 + p)
            arrive(part(p, x, za), w_dn + 2 * i - 2 + p)
            if i < 3:
                send(part(p, x, zb), w_up + 2 * i + p, z_up)
                send(part(p, x, za), w_dn + 2 * i + p, z_dn)
            elif p == 0:
                send(wb.at[0, x, 0, zb], w_up + 6, z_up)
                send(wb.at[0, x, 1, za], w_dn + 6, z_dn)
            else:
                send(part(1, x, zb), w_up + 7, z_up)
        if i == 0:
            weight_x(0)
        elif i < 4:
            weight_x(2 * i - 1)
            weight_x(2 * i)
        else:
            arrive(wb.at[0, x, 0, zb], w_up + 6)
            arrive(wb.at[0, x, 1, za], w_dn + 6)
            arrive(part(1, x, zb), w_up + 7)
            weight_x(7)

    xl, xr, xf = (x + 3) % 4, (x + 1) % 4, (x + 2) % 4
    low = z < 4

    def weight_x2(n):
        for p in range(2):
            arrive(part(p, xl, z_of(n)), x_up_ch + 2 * n + p)
            arrive(part(p, xr, z_of(n)), x_dn_ch + 2 * n + p)
            send(part(p, xl, z_of(n)), x2_ch + 2 * n + p, x_up, z >= 4)
            send(part(p, xr, z_of(n)), x2_ch + 2 * n + p, x_dn, low)

    def weight_y(n):
        xx = (x, xl, xr, xf)[n]
        if n == 3:
            for m in range(8):
                for p in range(2):
                    arrive(part(p, xf, z_of(m)), x2_ch + 2 * m + p)
        send(wb.at[1, xx, y], wy_ch + n, y_flip)

    qt = channel(4)

    def query_out():
        for d in range(1, GROUPS):
            col = pl.multiple_of(((g + d) % GROUPS) * WIDTH, HD)
            send(q_in.at[:, pl.ds(col, WIDTH)], q_ch + d, peer(d), dst=qb.at[0, pl.ds(row0, 32)])

    def query_time():
        for d in range(1, GROUPS):
            src_row = pl.multiple_of(((g + GROUPS - d) % GROUPS) * 32, 32)
            arrive(qb.at[0, pl.ds(src_row, 32)], q_ch + d)
        send(qb.at[0], qt, t_up, later, dst=qb.at[1])
        send(bb.at[0], qt + 1, t_up, later, dst=bb.at[1])
        send(qb.at[0], qt + 2, t_dn, earlier, dst=qb.at[2])
        send(bb.at[0], qt + 3, t_dn, earlier, dst=bb.at[2])

    def weight_pair():
        send(wb.at[0, x, y, z], w_y, y_flip)

    do(weight_pair)
    do(own_block, 0)
    do(query_out)
    arrive(wb.at[0, x, 1 - y, z], w_y)
    do(weight_z, 0)
    do(own_block, 1)
    do(weight_z, 1)
    do(ring, 1, 0)
    do(query_time)
    do(weight_z, 2)
    do(weight_x2, 0)
    do(ring, 2, 0)
    do(weight_z, 3)
    do(own_block, 2)
    do(weight_x2, 1)
    do(weight_x2, 2)
    do(ring, 1, 1)
    do(ring, 3, 0)
    do(weight_z, 4)
    do(weight_y, 0)
    do(ring, 1, 2)
    do(weight_x2, 3)
    do(weight_x2, 4)
    do(ring, 2, 1)
    do(ring, 4, 0)
    do(weight_x2, 5)
    do(weight_x2, 6)
    do(ring, 3, 1)
    do(ring, 2, 2)

    h_at = [h - (h + 3) // 4, h, h + 1 - h // 3]
    w_at = [w - (w + 3) // 4, w, w + 1 - w // 3]
    slots = [h_at[n // 3] * 4 + w_at[n % 3] for n in range(9)]
    lane = lax.broadcasted_iota(jnp.int32, (TILE, HD), 1)

    def unit(i, a):
        first = (9, 18, 0)[i]
        q = qb[i, :, pl.ds(pl.multiple_of(a * HD, HD), HD)]
        m = jnp.full((TILE, HD), NEG, jnp.float32)
        for n in range(9):
            sc = lax.dot_general(q, kv[slots[n], a, 0], (((1,), (1,)), ((), ())),
                                 preferred_element_type=jnp.float32)
            sb[n] = sc
            m = jnp.maximum(m, jnp.maximum(sc[:, :HD], sc[:, HD:]) - bb[i, first + n : first + n + 1, :])
        m = jnp.max(m, axis=1, keepdims=True) * SCALE
        ones = jnp.ones((TILE, HD), jnp.bfloat16)
        acc = jnp.zeros((TILE, 2 * HD), jnp.float32)
        for n in range(9):
            shift = m + bb[i, first + n : first + n + 1, :]
            p = jnp.exp2(sb[n] * SCALE - jnp.concatenate([shift, shift], axis=1))
            v = jnp.concatenate([kv[slots[n], a, 1], ones], axis=1)
            acc = acc + jnp.dot(p.astype(jnp.bfloat16), v, preferred_element_type=jnp.float32)
        return m, acc

    po_ch, ps_ch = channel(6), channel(6)
    a_ch, c_ch = channel(9), channel(12)
    edge = ((1, earlier, t_dn), (2, later, t_up))

    def missing(k, cond):
        @pl.when(cond)
        def _():
            rs[k] = jnp.full((HEADS_DEV, 8, TILE), NEG, jnp.float32)
            ro[k] = jnp.zeros((HEADS_DEV, TILE, HD), jnp.bfloat16)

    missing(0, t == 0)
    missing(1, t == 3)

    def back(k, a, dev):
        return (copy(po.at[k, a], ro.at[1 - k, a], po_ch + 3 * k + a, dev),
                copy(ps.at[k, a], rs.at[1 - k, a], ps_ch + 3 * k + a, dev))

    def feature(gg, a):
        return ab.at[:, pl.ds(pl.multiple_of(gg * WIDTH + a * HD, HD), HD)]

    def remote_unit(j, a):
        i, cond, dev = edge[j]

        @pl.when(cond)
        def _():
            m, acc = unit(i, a)
            k = i - 1
            po[k, a] = acc[:, :HD].astype(jnp.bfloat16)
            stat = jnp.where(lane == 0, m, acc[:, HD:])
            ps[k, a] = stat.T[:8]
            for c in back(k, a, dev):
                c.start()

    def own_unit(a):
        m, acc = unit(0, a)
        lo[a % 2] = acc
        ls[a % 2] = jnp.broadcast_to(m, (TILE, HD))

    def share(gg, a, ch, dev):
        return copy(feature(gg, a), feature(gg, a), ch, dev)

    def finish(a):
        for k, cond in ((0, earlier), (1, later)):
            @pl.when(cond)
            def _(k=k):
                copy(ro.at[k, a], ro.at[k, a], po_ch + 3 * (1 - k) + a, t_up).wait_recv()
                copy(rs.at[k, a], rs.at[k, a], ps_ch + 3 * (1 - k) + a, t_up).wait_recv()
        m0, num0, den0 = ls[a % 2][:, :1], lo[a % 2, :, :HD], lo[a % 2, :, HD:]
        stats = []
        for k in range(2):
            r = rs[k, a]
            st = jnp.concatenate([r] * 16, axis=0).T
            stats.append((st[:, :1], st[:, 1:2]))
        top = jnp.maximum(m0, jnp.maximum(stats[0][0], stats[1][0]))
        f0 = jnp.exp2(m0 - top)
        num, den = num0 * f0, den0 * f0
        for k in range(2):
            mk, lk = stats[k]
            f = jnp.exp2(mk - top)
            num = num + ro[k, a].astype(jnp.float32) * f
            den = den + jnp.maximum(lk, 0.0) * f
        feature(g, a)[...] = (num / den).astype(jnp.bfloat16)
        for d in range(1, 4):
            share(g, a, a_ch + 3 * (d - 1) + a, peer(2 * d)).start()
        share(g, a, c_ch + a, partner).start()

    def relay(a):
        for d in range(1, 4):
            src = (g + GROUPS - 2 * d) % GROUPS
            copy(feature(src, a), feature(src, a), a_ch + 3 * (d - 1) + a, z_up).wait_recv()
            share(src, a, c_ch + 3 * d + a, partner).start()

    arrive(qb.at[1], qt, earlier)
    arrive(bb.at[1], qt + 1, earlier)
    arrive(qb.at[2], qt + 2, later)
    arrive(bb.at[2], qt + 3, later)

    facing = z // 4 != x % 2
    up_face = jnp.logical_and(facing, w < 3)
    dn_face = jnp.logical_and(facing, w > 0)

    def crossed(a):
        arrive(kv.at[8 - base + (z + 5) % 8, a], e_ch + 3 + a, up_face)
        arrive(kv.at[8 - base + (z + 3) % 8, a], e_ch + 6 + a, dn_face)
        arrive(kv.at[8 - base + (z + 4) % 8, a], e_ch + a, facing)

    def head_step(a, _):
        crossed(a)
        remote_unit(0, a)

        @pl.when(a == 0)
        def _():
            do(ring, 4, 1)

        remote_unit(1, a)

        @pl.when(a == 0)
        def _():
            do(ring, 3, 2)
            do(weight_x2, 7)

        @pl.when(a > 0)
        def _():
            finish(a - 1)

        own_unit(a)

        @pl.when(a == 0)
        def _():
            do(ring, 4, 2)
            do(weight_y, 1)
            do(weight_y, 2)

        @pl.when(a == 1)
        def _():
            do(weight_y, 3)

        @pl.when(a == 2)
        def _():
            relay(0)

        return 0

    lax.fori_loop(0, HEADS_DEV, head_step, 0)
    finish(HEADS_DEV - 1)
    relay(1)
    for n, xx in enumerate((x, xl, xr, xf)):
        arrive(wb.at[1, xx, 1 - y], wy_ch + n)
    relay(2)
    for a in range(HEADS_DEV):
        for d in range(4):
            src = (g + 1 - 2 * core + GROUPS - 2 * d) % GROUPS
            copy(feature(src, a), feature(src, a), c_ch + 3 * d + a, z_up).wait_recv()

    for n in range(3):
        acc = jnp.zeros((TILE, 256), jnp.float32)
        for j in range(GROUPS):
            if n == 1:
                rows = jnp.concatenate([wb[0, j % 4, j // 4, :, :, 256:], wb[1, j % 4, j // 4, :, :, :128]], axis=2)
            else:
                rows = wb[n // 2, j % 4, j // 4, :, :, (0, 0, 128)[n] : (256, 0, 384)[n]]
            acc = acc + jnp.dot(ab[:, j * WIDTH : (j + 1) * WIDTH], rows.reshape(WIDTH, 256),
                                preferred_element_type=jnp.float32)
        out_ref[:, n * 256 : n * 256 + 256] = acc.astype(jnp.bfloat16)

    draining[0] = True
    for step, which in done:
        step(*which)
    for a in range(HEADS_DEV):
        for i, cond, dev in edge:
            for c in back(i - 1, a, dev):
                pl.when(cond)(c.wait_send)
        for d in range(1, 4):
            share(g, a, a_ch + 3 * (d - 1) + a, peer(2 * d)).wait_send()
        for d in range(4):
            share(g, a, c_ch + 3 * d + a, partner).wait_send()
    assert channels[0] <= N_CH


def local(queries, keys, values, window, out_weight):
    any_spec = pl.BlockSpec(memory_space=pl.ANY)
    bf16, f32 = jnp.bfloat16, jnp.float32
    return pl.pallas_call(
        kernel,
        out_shape=jax.ShapeDtypeStruct((TILE, out_weight.shape[1]), bf16),
        in_specs=[any_spec] * 3 + [pl.BlockSpec(memory_space=pltpu.SMEM), any_spec],
        out_specs=pl.BlockSpec(memory_space=pltpu.VMEM),
        scratch_shapes=[
            pltpu.VMEM((16, HEADS_DEV, 2, TILE, HD), bf16),
            pltpu.VMEM((2, 4, 2, 8, 48, WIDTH), bf16),
            pltpu.VMEM((3, TILE, WIDTH), bf16),
            pltpu.VMEM((3, 32, HD), f32),
            pltpu.VMEM((TILE, GROUPS * WIDTH), bf16),
            pltpu.VMEM((9, TILE, TILE), f32),
            pltpu.VMEM((2, HEADS_DEV, TILE, HD), bf16),
            pltpu.VMEM((2, HEADS_DEV, 8, TILE), f32),
            pltpu.VMEM((2, HEADS_DEV, TILE, HD), bf16),
            pltpu.VMEM((2, HEADS_DEV, 8, TILE), f32),
            pltpu.VMEM((2, TILE, 2 * HD), f32),
            pltpu.VMEM((2, TILE, HD), f32),
            pltpu.SemaphoreType.DMA((N_CH,)),
            pltpu.SemaphoreType.DMA((N_CH,)),
            pltpu.SemaphoreType.DMA((9,)),
        ],
        compiler_params=pltpu.CompilerParams(
            collective_id=0, has_side_effects=True, vmem_limit_bytes=60 * 1024 * 1024),
    )(queries, keys, values, window, out_weight)


def solution(mesh):
    in_specs = (
        P(("seq", "head"), None),
        P("seq", "head"),
        P("seq", "head"),
        P("seq", None),
        P("seq", "head"),
    )
    return jax.shard_map(local, mesh=mesh, in_specs=in_specs, out_specs=P("seq", "head"), check_vma=False)
```

```python
import functools

import jax
import jax.numpy as jnp
from jax import lax
from jax.experimental import pallas as pl
from jax.experimental.pallas import tpu as pltpu
from jax.sharding import PartitionSpec as P

MESH = pl.DeviceIdType.MESH
TILE = 256
HD = 128
HEADS_DEV = 3
WIDTH = HD * HEADS_DEV
GROUPS = 8
NEG = -1e30
BIG = 1e30
SCALE = 1.4426950408889634 * HD**-0.5
N_CH = 108


def kernel(q_in, k_in, v_in, win, w_in, out_ref,
           kv, wb, w2, wf, qb, bb, ab, sb, po, ps, ro, rs, lo, ls, send_sem, recv_sem, loc_sem):
    s = lax.axis_index("seq")
    g = lax.axis_index("head")
    y = s // 32
    x = (s // 8) % 4
    z = s % 8
    t = 2 * y + x // 2
    h = 2 * (x % 2) + z // 4
    w = z % 4
    core = g % 2

    def at(yy, xx, zz):
        return (yy * 32 + xx * 8 + zz, g)

    def at_time(tt):
        return (16 * tt + s % 16, g)

    z_up, z_dn = at(y, x, (z + 1) % 8), at(y, x, (z + 7) % 8)
    x_up, x_dn = at(y, (x + 1) % 4, z), at(y, (x + 3) % 4, z)
    x_flip = at(y, x + 1 - 2 * (x % 2), z)
    y_flip = at(1 - y, x, z)
    t_up, t_dn = at_time((t + 1) % 4), at_time((t + 3) % 4)
    partner = (s, g + 1 - 2 * core)

    def peer(d):
        return (s, (g + d) % GROUPS)

    barrier = pltpu.get_barrier_semaphore()
    greeted = [z_up, z_dn, x_up, x_dn, y_flip, t_up, t_dn] + [peer(d) for d in range(1, GROUPS)]
    for other in greeted:
        pl.semaphore_signal(barrier, inc=1, device_id=other, device_id_type=MESH)

    channels = [0]
    draining = [False]
    done = {}

    def channel(n=1):
        channels[0] += n
        return channels[0] - n

    def copy(src, dst, ch, dev):
        return pltpu.make_async_remote_copy(
            src_ref=src, dst_ref=dst, send_sem=send_sem.at[ch], recv_sem=recv_sem.at[ch],
            device_id=dev, device_id_type=MESH)

    def send(ref, ch, dev, cond=None, dst=None):
        c = copy(ref, ref if dst is None else dst, ch, dev)
        act = c.wait_send if draining[0] else c.start
        if cond is None:
            act()
        else:
            pl.when(cond)(act)

    def do(step, *which):
        step(*which)
        done[step, which] = None

    def arrive(dst, ch, cond=None):
        if draining[0]:
            return
        c = copy(dst, dst, ch, z_up)
        if cond is None:
            c.wait_recv()
        else:
            pl.when(cond)(c.wait_recv)

    base = 8 * (x % 2)
    own = base + z
    row0 = pl.multiple_of(g * 32, 32)
    col0 = pl.multiple_of(g * WIDTH, HD)
    local = []
    for a in range(HEADS_DEV):
        cols = pl.ds(a * HD, HD)
        local.append(pltpu.make_async_copy(k_in.at[:, cols], kv.at[own, a, 0], loc_sem.at[2 * a]))
        local.append(pltpu.make_async_copy(v_in.at[:, cols], kv.at[own, a, 1], loc_sem.at[2 * a + 1]))
    local.append(pltpu.make_async_copy(w_in.at[:, pl.ds(0, WIDTH)], wb.at[x, z, y], loc_sem.at[6]))
    local.append(pltpu.make_async_copy(w_in.at[:, pl.ds(WIDTH, WIDTH)], w2.at[z, x], loc_sem.at[7]))
    local.append(pltpu.make_async_copy(q_in.at[:, pl.ds(col0, WIDTH)], qb.at[0, pl.ds(row0, 32)], loc_sem.at[8]))
    for c in local:
        c.start()
    for n in range(27):
        bb[0, n : n + 1, :] = jnp.full((1, HD), jnp.where(win[0, n] >= 0, 0.0, BIG), jnp.float32)
    for c in local:
        c.wait()
    pl.semaphore_wait(barrier, len(greeted))

    up, dn = channel(12) - 3, channel(12) - 3
    e_ch = channel(9)
    q_ch = channel()
    w_y = channel()
    w_up, w_dn = channel(4), channel(4)
    x_up_ch, x_dn_ch, x2_ch = channel(8), channel(8), channel(8)
    wy_ch, p_up, p_dn, p_x2 = channel(), channel(), channel(), channel()
    pz_up, pz_dn = channel(4), channel(4)
    later, earlier = t < 3, t > 0

    def own_block(a):
        send(kv.at[own, a], up + 3 + a, z_up)
        send(kv.at[own, a], dn + 3 + a, z_dn)

    crossing = z // 4 == x % 2
    up_edge = jnp.logical_and(crossing, w < 3)
    dn_edge = jnp.logical_and(crossing, w > 0)

    def ring(i, a):
        below, above = base + (z + 8 - i) % 8, base + (z + i) % 8
        wb_, wa_ = (w + 8 - i) % 4, (w + i) % 4
        if i == 4:
            arrive(kv.at[below, a], up + 3 * i + a, w >= 2)
            arrive(kv.at[below, a], dn + 3 * i + a, w < 2)
            send(kv.at[below, a], e_ch + a, x_flip, crossing)
            return
        arrive(kv.at[below, a], up + 3 * i + a, None if i == 1 else wb_ > 0)
        send(kv.at[below, a], up + 3 * i + 3 + a, z_up, wb_ > (0 if i < 3 else 1))
        if i == 3:
            send(kv.at[below, a], e_ch + 3 + a, x_flip, up_edge)
        arrive(kv.at[above, a], dn + 3 * i + a, None if i == 1 else wa_ < 3)
        send(kv.at[above, a], dn + 3 * i + 3 + a, z_dn, wa_ < (3 if i < 3 else 2))
        if i == 3:
            send(kv.at[above, a], e_ch + 6 + a, x_flip, dn_edge)

    def z_of(n):
        return (z + 8 - (n + 1) // 2) % 8 if n % 2 else (z + n // 2) % 8

    xl, xr, xf = (x + 3) % 4, (x + 1) % 4, (x + 2) % 4

    def start(src, dst, ch, dev):
        if not draining[0]:
            copy(src, dst, ch, dev).start()

    def weight_y(n):
        start(w2.at[z_of(n)], wf.at[z_of(n)], wy_ch, y_flip)

    def weight_x(n):
        block = wb.at[x, z_of(n)]
        send(block, x_up_ch + n, x_up)
        send(block, x_dn_ch + n, x_dn)

    def weight_z(i):
        if i == 0:
            send(wb.at[x, z], w_up, z_up)
            send(wb.at[x, z], w_dn, z_dn)
            weight_x(0)
            return
        below, above = wb.at[x, (z + 8 - i) % 8], wb.at[x, (z + i) % 8]
        if i == 4:
            arrive(below.at[0], w_up + 3)
            arrive(below.at[1], w_dn + 3)
            weight_x(7)
            return
        arrive(below, w_up + i - 1)
        arrive(above, w_dn + i - 1)
        if i < 3:
            send(below, w_up + i, z_up)
            send(above, w_dn + i, z_dn)
        else:
            send(below.at[0], w_up + i, z_up)
            send(above.at[1], w_dn + i, z_dn)
        weight_x(2 * i - 1)
        weight_x(2 * i)

    def weight_x2(n):
        from_l, from_r = wb.at[xl, z_of(n)], wb.at[xr, z_of(n)]
        arrive(from_l, x_up_ch + n)
        arrive(from_r, x_dn_ch + n)
        if n % 2:
            send(from_r, x2_ch + n, x_dn)
        else:
            send(from_l, x2_ch + n, x_up, z >= 4)
            send(from_r, x2_ch + n, x_dn, z < 4)

    def second_x():
        send(w2.at[z, x], p_up, x_up)
        send(w2.at[z, x], p_dn, x_dn)

    def second_x2():
        arrive(w2.at[z, xl], p_up)
        arrive(w2.at[z, xr], p_dn)
        send(w2.at[z, xl], p_x2, x_up)

    def second_z(i):
        below, above = w2.at[(z + 8 - i) % 8], w2.at[(z + i) % 8]
        if i == 0:
            arrive(w2.at[z, xf], p_x2)
            send(below, pz_up, z_up)
            send(below, pz_dn, z_dn)
            weight_y(0)
            return
        if i == 4:
            arrive(below.at[pl.ds(0, 2)], pz_up + 3)
            arrive(below.at[pl.ds(2, 2)], pz_dn + 3)
            weight_y(7)
            return
        arrive(below, pz_up + i - 1)
        arrive(above, pz_dn + i - 1)
        send(below if i < 3 else below.at[pl.ds(0, 2)], pz_up + i, z_up)
        send(above if i < 3 else above.at[pl.ds(2, 2)], pz_dn + i, z_dn)
        weight_y(2 * i - 1)
        weight_y(2 * i)

    qt = channel(4)

    def query_out():
        for d in range(1, GROUPS):
            col = pl.multiple_of(((g + d) % GROUPS) * WIDTH, HD)
            start(q_in.at[:, pl.ds(col, WIDTH)], qb.at[0, pl.ds(row0, 32)], q_ch, peer(d))

    def query_time():
        arrive(qb.at[0, pl.ds(0, 224)], q_ch)
        send(qb.at[0], qt, t_up, later, dst=qb.at[1])
        send(bb.at[0], qt + 1, t_up, later, dst=bb.at[1])
        send(qb.at[0], qt + 2, t_dn, earlier, dst=qb.at[2])
        send(bb.at[0], qt + 3, t_dn, earlier, dst=bb.at[2])

    def weight_pair():
        send(wb.at[x, z, y], w_y, y_flip)

    do(weight_pair)
    do(second_x)
    do(own_block, 0)
    do(query_out)
    arrive(wb.at[x, z, 1 - y], w_y)
    do(weight_z, 0)
    do(second_x2)
    do(own_block, 1)
    do(weight_z, 1)
    do(ring, 1, 0)
    do(query_time)
    do(weight_z, 2)
    do(weight_x2, 0)
    do(ring, 2, 0)
    do(weight_z, 3)
    do(own_block, 2)
    do(second_z, 0)
    do(weight_x2, 1)
    do(weight_x2, 2)
    do(ring, 1, 1)
    do(ring, 3, 0)
    do(weight_z, 4)
    do(ring, 1, 2)
    do(weight_x2, 3)
    do(ring, 2, 1)
    do(ring, 4, 0)
    do(weight_x2, 4)
    do(second_z, 1)
    do(ring, 3, 1)
    do(ring, 2, 2)
    do(weight_x2, 5)
    do(weight_x2, 6)

    h_at = [h - (h + 3) // 4, h, h + 1 - h // 3]
    w_at = [w - (w + 3) // 4, w, w + 1 - w // 3]
    slots = [h_at[n // 3] * 4 + w_at[n % 3] for n in range(9)]
    lane = lax.broadcasted_iota(jnp.int32, (TILE, HD), 1)

    def unit(i, a):
        first = (9, 18, 0)[i]
        q = qb[i, :, pl.ds(pl.multiple_of(a * HD, HD), HD)]
        m = jnp.full((TILE, HD), NEG, jnp.float32)
        for n in range(9):
            sc = lax.dot_general(q, kv[slots[n], a, 0], (((1,), (1,)), ((), ())),
                                 preferred_element_type=jnp.float32)
            sb[n] = sc
            m = jnp.maximum(m, jnp.maximum(sc[:, :HD], sc[:, HD:]) - bb[i, first + n : first + n + 1, :])
        m = jnp.max(m, axis=1, keepdims=True) * SCALE
        ones = jnp.ones((TILE, HD), jnp.bfloat16)
        acc = jnp.zeros((TILE, 2 * HD), jnp.float32)
        for n in range(9):
            shift = m + bb[i, first + n : first + n + 1, :]
            p = jnp.exp2(sb[n] * SCALE - jnp.concatenate([shift, shift], axis=1))
            v = jnp.concatenate([kv[slots[n], a, 1], ones], axis=1)
            acc = acc + jnp.dot(p.astype(jnp.bfloat16), v, preferred_element_type=jnp.float32)
        return m, acc

    po_ch, ps_ch = channel(6), channel(6)
    a_up, a_dn, far_up, far_dn, c_ch = channel(3), channel(3), channel(3), channel(3), channel()
    edge = ((1, earlier, t_dn), (2, later, t_up))

    def missing(k, cond):
        @pl.when(cond)
        def _():
            rs[k] = jnp.full((HEADS_DEV, 8, TILE), NEG, jnp.float32)
            ro[k] = jnp.zeros((HEADS_DEV, TILE, HD), jnp.bfloat16)

    missing(0, t == 0)
    missing(1, t == 3)

    def back(k, a, dev):
        return (copy(po.at[k, a], ro.at[1 - k, a], po_ch + 3 * k + a, dev),
                copy(ps.at[k, a], rs.at[1 - k, a], ps_ch + 3 * k + a, dev))

    def feature(gg, a):
        return ab.at[HEADS_DEV * gg + a]

    def remote_unit(j, a):
        i, cond, dev = edge[j]

        @pl.when(cond)
        def _():
            m, acc = unit(i, a)
            k = i - 1
            po[k, a] = acc[:, :HD].astype(jnp.bfloat16)
            stat = jnp.where(lane == 0, m, acc[:, HD:])
            ps[k, a] = stat.T[:8]
            for c in back(k, a, dev):
                c.start()

    def own_unit(a):
        m, acc = unit(0, a)
        lo[a % 2] = acc
        ls[a % 2] = jnp.broadcast_to(m, (TILE, HD))

    def share(gg, a, ch, dev):
        return copy(feature(gg, a), feature(gg, a), ch, dev)

    def finish(a):
        for k, cond in ((0, earlier), (1, later)):
            @pl.when(cond)
            def _(k=k):
                copy(ro.at[k, a], ro.at[k, a], po_ch + 3 * (1 - k) + a, t_up).wait_recv()
                copy(rs.at[k, a], rs.at[k, a], ps_ch + 3 * (1 - k) + a, t_up).wait_recv()
        m0, num0, den0 = ls[a % 2][:, :1], lo[a % 2, :, :HD], lo[a % 2, :, HD:]
        stats = []
        for k in range(2):
            r = rs[k, a]
            st = jnp.concatenate([r] * 16, axis=0).T
            stats.append((st[:, :1], st[:, 1:2]))
        top = jnp.maximum(m0, jnp.maximum(stats[0][0], stats[1][0]))
        f0 = jnp.exp2(m0 - top)
        num, den = num0 * f0, den0 * f0
        for k in range(2):
            mk, lk = stats[k]
            f = jnp.exp2(mk - top)
            num = num + ro[k, a].astype(jnp.float32) * f
            den = den + jnp.maximum(lk, 0.0) * f
        feature(g, a)[...] = (num / den).astype(jnp.bfloat16)
        for c in near(g, g, a):
            c.start()
        share(g, a, c_ch, partner).start()

    def near(lower, upper, a):
        return share(lower, a, a_up + a, peer(2)), share(upper, a, a_dn + a, peer(6))

    def halves(lower, upper, a):
        top, bottom = feature(lower, a).at[pl.ds(0, HD)], feature(upper, a).at[pl.ds(HD, HD)]
        return copy(top, top, far_up + a, peer(2)), copy(bottom, bottom, far_dn + a, peer(6))

    lower, upper, farther = (g + 6) % GROUPS, (g + 2) % GROUPS, (g + 4) % GROUPS

    def relay_near(a):
        for gg, came, on in zip((lower, upper), near(lower, upper, a), halves(lower, upper, a)):
            came.wait_recv()
            on.start()
            share(gg, a, c_ch, partner).start()

    def relay_far(a):
        for came in halves(farther, farther, a):
            came.wait_recv()
        share(farther, a, c_ch, partner).start()

    arrive(qb.at[1], qt, earlier)
    arrive(bb.at[1], qt + 1, earlier)
    arrive(qb.at[2], qt + 2, later)
    arrive(bb.at[2], qt + 3, later)

    facing = z // 4 != x % 2
    up_face = jnp.logical_and(facing, w < 3)
    dn_face = jnp.logical_and(facing, w > 0)

    def crossed(a):
        arrive(kv.at[8 - base + (z + 5) % 8, a], e_ch + 3 + a, up_face)
        arrive(kv.at[8 - base + (z + 3) % 8, a], e_ch + 6 + a, dn_face)
        arrive(kv.at[8 - base + (z + 4) % 8, a], e_ch + a, facing)

    def head_step(a, _):
        crossed(a)
        remote_unit(0, a)

        @pl.when(a == 0)
        def _():
            do(second_z, 2)
            do(ring, 4, 1)

        @pl.when(a == 1)
        def _():
            do(ring, 4, 2)

        remote_unit(1, a)

        @pl.when(a == 0)
        def _():
            do(ring, 3, 2)
            do(weight_x2, 7)
            do(second_z, 3)

        @pl.when(a > 0)
        def _():
            finish(a - 1)

        @pl.when(a == 1)
        def _():
            do(second_z, 4)

        @pl.when(a == 2)
        def _():
            relay_near(0)

        own_unit(a)

        return 0

    lax.fori_loop(0, HEADS_DEV, head_step, 0)
    relay_near(1)
    finish(HEADS_DEV - 1)
    relay_far(0)
    relay_far(1)
    for n in range(8):
        arrive(wb.at[xf, z_of(n)], x2_ch + n)
    arrive(wf, wy_ch)
    relay_near(2)
    relay_far(2)
    twelve = ab.at[pl.ds(0, 12)]
    copy(twelve, twelve, c_ch, z_up).wait_recv()

    def wide(gg):
        return jnp.concatenate([ab[HEADS_DEV * gg + a] for a in range(HEADS_DEV)], axis=1)

    for half in range(2):
        acc = jnp.zeros((TILE, WIDTH), jnp.float32)
        for j in range(4):
            for k in range(2):
                if half == 0:
                    left, rows = wide(4 * k + j), wb[j, :, k]
                elif k == 0:
                    left, rows = wide(4 * y + j), w2[:, j]
                else:
                    left, rows = wide(4 - 4 * y + j), wf[:, j]
                acc = acc + jnp.dot(left, rows.reshape(WIDTH, WIDTH), preferred_element_type=jnp.float32)
        out_ref[:, half * WIDTH : (half + 1) * WIDTH] = acc.astype(jnp.bfloat16)

    draining[0] = True
    for step, which in done:
        step(*which)
    for a in range(HEADS_DEV):
        for i, cond, dev in edge:
            for c in back(i - 1, a, dev):
                pl.when(cond)(c.wait_send)
        for c in near(g, g, a) + halves(lower, upper, a):
            c.wait_send()
    copy(twelve, twelve, c_ch, partner).wait_send()
    copy(wf, wf, wy_ch, y_flip).wait_send()
    sevenths = qb.at[0, pl.ds(0, 224)]
    copy(sevenths, sevenths, q_ch, partner).wait_send()
    assert channels[0] == N_CH, channels[0]


def local(queries, keys, values, window, out_weight):
    any_spec = pl.BlockSpec(memory_space=pl.ANY)
    bf16, f32 = jnp.bfloat16, jnp.float32
    return pl.pallas_call(
        kernel,
        out_shape=jax.ShapeDtypeStruct((TILE, out_weight.shape[1]), bf16),
        in_specs=[any_spec] * 3 + [pl.BlockSpec(memory_space=pltpu.SMEM), any_spec],
        out_specs=pl.BlockSpec(memory_space=pltpu.VMEM),
        scratch_shapes=[
            pltpu.VMEM((16, HEADS_DEV, 2, TILE, HD), bf16),
            pltpu.VMEM((4, 8, 2, 48, WIDTH), bf16),
            pltpu.VMEM((8, 4, 48, WIDTH), bf16),
            pltpu.VMEM((8, 4, 48, WIDTH), bf16),
            pltpu.VMEM((3, TILE, WIDTH), bf16),
            pltpu.VMEM((3, 32, HD), f32),
            pltpu.VMEM((GROUPS * HEADS_DEV, TILE, HD), bf16),
            pltpu.VMEM((9, TILE, TILE), f32),
            pltpu.VMEM((2, HEADS_DEV, TILE, HD), bf16),
            pltpu.VMEM((2, HEADS_DEV, 8, TILE), f32),
            pltpu.VMEM((2, HEADS_DEV, TILE, HD), bf16),
            pltpu.VMEM((2, HEADS_DEV, 8, TILE), f32),
            pltpu.VMEM((2, TILE, 2 * HD), f32),
            pltpu.VMEM((2, TILE, HD), f32),
            pltpu.SemaphoreType.DMA((N_CH,)),
            pltpu.SemaphoreType.DMA((N_CH,)),
            pltpu.SemaphoreType.DMA((9,)),
        ],
        compiler_params=pltpu.CompilerParams(
            collective_id=0, has_side_effects=True, vmem_limit_bytes=60 * 1024 * 1024),
    )(queries, keys, values, window, out_weight)


def solution(mesh):
    in_specs = (
        P(("seq", "head"), None),
        P("seq", "head"),
        P("seq", "head"),
        P("seq", None),
        P("seq", "head"),
    )
    return jax.shard_map(local, mesh=mesh, in_specs=in_specs, out_specs=P("seq", "head"), check_vma=False)
```

```python
import functools

import jax
import jax.numpy as jnp
from jax import lax
from jax.experimental import pallas as pl
from jax.experimental.pallas import tpu as pltpu
from jax.sharding import PartitionSpec as P

MESH = pl.DeviceIdType.MESH
TILE = 256
HD = 128
HEADS_DEV = 3
WIDTH = HD * HEADS_DEV
GROUPS = 8
NEG = -1e30
BIG = 1e30
SCALE = 1.4426950408889634 * HD**-0.5
N_CH = 109


def kernel(q_in, k_in, v_in, win, w_in, out_ref,
           kv, wb, w2, wf, qb, bb, ab, sb, po, ps, ro, rs, lo, ls, part_sum, send_sem, recv_sem, loc_sem):
    s = lax.axis_index("seq")
    g = lax.axis_index("head")
    y = s // 32
    x = (s // 8) % 4
    z = s % 8
    t = 2 * y + x // 2
    h = 2 * (x % 2) + z // 4
    w = z % 4
    core = g % 2

    def at(yy, xx, zz):
        return (yy * 32 + xx * 8 + zz, g)

    def at_time(tt):
        return (16 * tt + s % 16, g)

    z_up, z_dn = at(y, x, (z + 1) % 8), at(y, x, (z + 7) % 8)
    x_up, x_dn = at(y, (x + 1) % 4, z), at(y, (x + 3) % 4, z)
    x_flip = at(y, x + 1 - 2 * (x % 2), z)
    y_flip = at(1 - y, x, z)
    t_up, t_dn = at_time((t + 1) % 4), at_time((t + 3) % 4)
    partner = (s, g + 1 - 2 * core)

    def peer(d):
        return (s, (g + d) % GROUPS)

    barrier = pltpu.get_barrier_semaphore()
    greeted = [z_up, z_dn, x_up, x_dn, y_flip, t_up, t_dn] + [peer(d) for d in range(1, GROUPS)]
    for other in greeted:
        pl.semaphore_signal(barrier, inc=1, device_id=other, device_id_type=MESH)

    channels = [0]
    draining = [False]
    done = {}

    def channel(n=1):
        channels[0] += n
        return channels[0] - n

    def copy(src, dst, ch, dev):
        return pltpu.make_async_remote_copy(
            src_ref=src, dst_ref=dst, send_sem=send_sem.at[ch], recv_sem=recv_sem.at[ch],
            device_id=dev, device_id_type=MESH)

    def send(ref, ch, dev, cond=None, dst=None):
        c = copy(ref, ref if dst is None else dst, ch, dev)
        act = c.wait_send if draining[0] else c.start
        if cond is None:
            act()
        else:
            pl.when(cond)(act)

    def do(step, *which):
        step(*which)
        done[step, which] = None

    def arrive(dst, ch, cond=None):
        if draining[0]:
            return
        c = copy(dst, dst, ch, z_up)
        if cond is None:
            c.wait_recv()
        else:
            pl.when(cond)(c.wait_recv)

    base = 8 * (x % 2)
    own = base + z
    row0 = pl.multiple_of(g * 32, 32)
    col0 = pl.multiple_of(g * WIDTH, HD)
    local = []
    for a in range(HEADS_DEV):
        cols = pl.ds(a * HD, HD)
        local.append(pltpu.make_async_copy(k_in.at[:, cols], kv.at[own, a, 0], loc_sem.at[2 * a]))
        local.append(pltpu.make_async_copy(v_in.at[:, cols], kv.at[own, a, 1], loc_sem.at[2 * a + 1]))
    local.append(pltpu.make_async_copy(w_in.at[:, pl.ds(0, WIDTH)], wb.at[x, z, y], loc_sem.at[6]))
    local.append(pltpu.make_async_copy(w_in.at[:, pl.ds(WIDTH, WIDTH)], w2.at[z, x], loc_sem.at[7]))
    local.append(pltpu.make_async_copy(q_in.at[:, pl.ds(col0, WIDTH)], qb.at[0, pl.ds(row0, 32)], loc_sem.at[8]))
    for c in local:
        c.start()
    pl.semaphore_wait(barrier, len(greeted))

    up, dn = channel(12) - 3, channel(12) - 3
    e_ch = channel(9)
    q_ch = channel()
    w_y = channel()
    w_up, w_dn = channel(4), channel(4)
    x_up_ch, x_dn_ch, x2_ch = channel(8), channel(8), channel(8)
    wy_ch, p_up, p_dn, p_x2 = channel(), channel(), channel(), channel()
    pz_up, pz_dn = channel(4), channel(4)
    later, earlier = t < 3, t > 0

    def own_block(a):
        send(kv.at[own, a], up + 3 + a, z_up)
        send(kv.at[own, a], dn + 3 + a, z_dn)

    crossing = z // 4 == x % 2
    up_edge = jnp.logical_and(crossing, w < 3)
    dn_edge = jnp.logical_and(crossing, w > 0)

    def ring(i, a):
        below, above = base + (z + 8 - i) % 8, base + (z + i) % 8
        wb_, wa_ = (w + 8 - i) % 4, (w + i) % 4
        if i == 4:
            arrive(kv.at[below, a], up + 3 * i + a, w >= 2)
            arrive(kv.at[below, a], dn + 3 * i + a, w < 2)
            send(kv.at[below, a], e_ch + a, x_flip, crossing)
            return
        arrive(kv.at[below, a], up + 3 * i + a, None if i == 1 else wb_ > 0)
        send(kv.at[below, a], up + 3 * i + 3 + a, z_up, wb_ > (0 if i < 3 else 1))
        if i == 3:
            send(kv.at[below, a], e_ch + 3 + a, x_flip, up_edge)
        arrive(kv.at[above, a], dn + 3 * i + a, None if i == 1 else wa_ < 3)
        send(kv.at[above, a], dn + 3 * i + 3 + a, z_dn, wa_ < (3 if i < 3 else 2))
        if i == 3:
            send(kv.at[above, a], e_ch + 6 + a, x_flip, dn_edge)

    def z_of(n):
        return (z + 8 - (n + 1) // 2) % 8 if n % 2 else (z + n // 2) % 8

    xl, xr, xf = (x + 3) % 4, (x + 1) % 4, (x + 2) % 4

    def start(src, dst, ch, dev):
        if not draining[0]:
            copy(src, dst, ch, dev).start()

    def weight_y(n):
        start(w2.at[z_of(n)], wf.at[z_of(n)], wy_ch, y_flip)

    def weight_x(n):
        block = wb.at[x, z_of(n)]
        send(block, x_up_ch + n, x_up)
        send(block, x_dn_ch + n, x_dn)

    def weight_z(i):
        if i == 0:
            send(wb.at[x, z], w_up, z_up)
            send(wb.at[x, z], w_dn, z_dn)
            weight_x(0)
            return
        below, above = wb.at[x, (z + 8 - i) % 8], wb.at[x, (z + i) % 8]
        if i == 4:
            arrive(below.at[0], w_up + 3)
            arrive(below.at[1], w_dn + 3)
            weight_x(7)
            return
        arrive(below, w_up + i - 1)
        arrive(above, w_dn + i - 1)
        if i < 3:
            send(below, w_up + i, z_up)
            send(above, w_dn + i, z_dn)
        else:
            send(below.at[0], w_up + i, z_up)
            send(above.at[1], w_dn + i, z_dn)
        weight_x(2 * i - 1)
        weight_x(2 * i)

    def weight_x2(n):
        from_l, from_r = wb.at[xl, z_of(n)], wb.at[xr, z_of(n)]
        arrive(from_l, x_up_ch + n)
        arrive(from_r, x_dn_ch + n)
        if n % 2:
            send(from_r, x2_ch + n, x_dn)
        else:
            send(from_l, x2_ch + n, x_up, z >= 4)
            send(from_r, x2_ch + n, x_dn, z < 4)

    def second_x():
        send(w2.at[z, x], p_up, x_up)
        send(w2.at[z, x], p_dn, x_dn)

    def second_x2():
        arrive(w2.at[z, xl], p_up)
        arrive(w2.at[z, xr], p_dn)
        send(w2.at[z, xl], p_x2, x_up)

    def second_z(i):
        below, above = w2.at[(z + 8 - i) % 8], w2.at[(z + i) % 8]
        if i == 0:
            arrive(w2.at[z, xf], p_x2)
            send(below, pz_up, z_up)
            send(below, pz_dn, z_dn)
            weight_y(0)
            return
        if i == 4:
            arrive(below.at[pl.ds(0, 2)], pz_up + 3)
            arrive(below.at[pl.ds(2, 2)], pz_dn + 3)
            weight_y(7)
            return
        arrive(below, pz_up + i - 1)
        arrive(above, pz_dn + i - 1)
        send(below if i < 3 else below.at[pl.ds(0, 2)], pz_up + i, z_up)
        send(above if i < 3 else above.at[pl.ds(2, 2)], pz_dn + i, z_dn)
        weight_y(2 * i - 1)
        weight_y(2 * i)

    qt = channel(4)

    def query_out():
        for d in range(1, GROUPS):
            col = pl.multiple_of(((g + d) % GROUPS) * WIDTH, HD)
            start(q_in.at[:, pl.ds(col, WIDTH)], qb.at[0, pl.ds(row0, 32)], q_ch, peer(d))

    def query_time():
        arrive(qb.at[0, pl.ds(0, 224)], q_ch)
        send(qb.at[0], qt, t_up, later, dst=qb.at[1])
        send(bb.at[0], qt + 1, t_up, later, dst=bb.at[1])
        send(qb.at[0], qt + 2, t_dn, earlier, dst=qb.at[2])
        send(bb.at[0], qt + 3, t_dn, earlier, dst=bb.at[2])

    def weight_pair():
        send(wb.at[x, z, y], w_y, y_flip)

    for c in local[:2]:
        c.wait()
    do(own_block, 0)
    for c in local[6:8]:
        c.wait()
    do(weight_pair)
    do(second_x)
    do(query_out)
    for n in range(27):
        bb[0, n : n + 1, :] = jnp.full((1, HD), jnp.where(win[0, n] >= 0, 0.0, BIG), jnp.float32)
    for c in local[2:6] + local[8:]:
        c.wait()
    arrive(wb.at[x, z, 1 - y], w_y)
    do(weight_z, 0)
    do(second_x2)
    do(own_block, 1)
    do(weight_z, 1)
    do(ring, 1, 0)
    do(query_time)
    do(weight_z, 2)
    do(weight_x2, 0)
    do(ring, 2, 0)
    do(weight_z, 3)
    do(own_block, 2)
    do(second_z, 0)
    do(weight_x2, 1)
    do(weight_x2, 2)
    do(ring, 1, 1)
    do(ring, 3, 0)
    do(weight_z, 4)
    do(ring, 1, 2)
    do(weight_x2, 3)
    do(ring, 2, 1)
    do(ring, 4, 0)
    do(weight_x2, 4)
    do(second_z, 1)
    do(ring, 3, 1)
    do(ring, 2, 2)
    do(weight_x2, 5)
    do(weight_x2, 6)

    h_at = [h - (h + 3) // 4, h, h + 1 - h // 3]
    w_at = [w - (w + 3) // 4, w, w + 1 - w // 3]
    slots = [h_at[n // 3] * 4 + w_at[n % 3] for n in range(9)]
    lane = lax.broadcasted_iota(jnp.int32, (TILE, HD), 1)

    def unit(i, a):
        first = (9, 18, 0)[i]
        q = qb[i, :, pl.ds(pl.multiple_of(a * HD, HD), HD)]
        m = jnp.full((TILE, HD), NEG, jnp.float32)
        for n in range(9):
            sc = lax.dot_general(q, kv[slots[n], a, 0], (((1,), (1,)), ((), ())),
                                 preferred_element_type=jnp.float32)
            sb[n] = sc
            m = jnp.maximum(m, jnp.maximum(sc[:, :HD], sc[:, HD:]) - bb[i, first + n : first + n + 1, :])
        m = jnp.max(m, axis=1, keepdims=True) * SCALE
        ones = jnp.ones((TILE, HD), jnp.bfloat16)
        acc = jnp.zeros((TILE, 2 * HD), jnp.float32)
        for n in range(9):
            shift = m + bb[i, first + n : first + n + 1, :]
            p = jnp.exp2(sb[n] * SCALE - jnp.concatenate([shift, shift], axis=1))
            v = jnp.concatenate([kv[slots[n], a, 1], ones], axis=1)
            acc = acc + jnp.dot(p.astype(jnp.bfloat16), v, preferred_element_type=jnp.float32)
        return m, acc

    po_ch, ps_ch = channel(6), channel(6)
    a_up, a_dn, far_up, far_dn, c_ch = channel(3), channel(3), channel(3), channel(3), channel(2)
    edge = ((1, earlier, t_dn), (2, later, t_up))

    def missing(k, cond):
        @pl.when(cond)
        def _():
            rs[k] = jnp.full((HEADS_DEV, 8, TILE), NEG, jnp.float32)
            ro[k] = jnp.zeros((HEADS_DEV, TILE, HD), jnp.bfloat16)

    missing(0, t == 0)
    missing(1, t == 3)

    def back(k, a, dev):
        return (copy(po.at[k, a], ro.at[1 - k, a], po_ch + 3 * k + a, dev),
                copy(ps.at[k, a], rs.at[1 - k, a], ps_ch + 3 * k + a, dev))

    def feature(gg, a):
        return ab.at[HEADS_DEV * gg + a]

    def remote_unit(j, a):
        i, cond, dev = edge[j]

        @pl.when(cond)
        def _():
            m, acc = unit(i, a)
            k = i - 1
            po[k, a] = acc[:, :HD].astype(jnp.bfloat16)
            stat = jnp.where(lane == 0, m, acc[:, HD:])
            ps[k, a] = stat.T[:8]
            for c in back(k, a, dev):
                c.start()

    def own_unit(a):
        m, acc = unit(0, a)
        lo[a % 2] = acc
        ls[a % 2] = jnp.broadcast_to(m, (TILE, HD))

    def share(gg, a, ch, dev):
        return copy(feature(gg, a), feature(gg, a), ch, dev)

    def finish(a):
        for k, cond in ((0, earlier), (1, later)):
            @pl.when(cond)
            def _(k=k):
                copy(ro.at[k, a], ro.at[k, a], po_ch + 3 * (1 - k) + a, t_up).wait_recv()
                copy(rs.at[k, a], rs.at[k, a], ps_ch + 3 * (1 - k) + a, t_up).wait_recv()
        m0, num0, den0 = ls[a % 2][:, :1], lo[a % 2, :, :HD], lo[a % 2, :, HD:]
        stats = []
        for k in range(2):
            r = rs[k, a]
            st = jnp.concatenate([r] * 16, axis=0).T
            stats.append((st[:, :1], st[:, 1:2]))
        top = jnp.maximum(m0, jnp.maximum(stats[0][0], stats[1][0]))
        f0 = jnp.exp2(m0 - top)
        num, den = num0 * f0, den0 * f0
        for k in range(2):
            mk, lk = stats[k]
            f = jnp.exp2(mk - top)
            num = num + ro[k, a].astype(jnp.float32) * f
            den = den + jnp.maximum(lk, 0.0) * f
        feature(g, a)[...] = (num / den).astype(jnp.bfloat16)
        for c in near(g, g, a):
            c.start()
        share(g, a, c_ch + a // 2, partner).start()

    def near(lower, upper, a):
        return share(lower, a, a_up + a, peer(2)), share(upper, a, a_dn + a, peer(6))

    def halves(lower, upper, a):
        top, bottom = feature(lower, a).at[pl.ds(0, HD)], feature(upper, a).at[pl.ds(HD, HD)]
        return copy(top, top, far_up + a, peer(2)), copy(bottom, bottom, far_dn + a, peer(6))

    lower, upper, farther = (g + 6) % GROUPS, (g + 2) % GROUPS, (g + 4) % GROUPS

    def relay_near(a):
        for gg, came, on in zip((lower, upper), near(lower, upper, a), halves(lower, upper, a)):
            came.wait_recv()
            on.start()
            share(gg, a, c_ch + a // 2, partner).start()

    def relay_far(a):
        for came in halves(farther, farther, a):
            came.wait_recv()
        share(farther, a, c_ch + a // 2, partner).start()

    arrive(qb.at[1], qt, earlier)
    arrive(bb.at[1], qt + 1, earlier)
    arrive(qb.at[2], qt + 2, later)
    arrive(bb.at[2], qt + 3, later)

    facing = z // 4 != x % 2
    up_face = jnp.logical_and(facing, w < 3)
    dn_face = jnp.logical_and(facing, w > 0)

    def crossed(a):
        arrive(kv.at[8 - base + (z + 5) % 8, a], e_ch + 3 + a, up_face)
        arrive(kv.at[8 - base + (z + 3) % 8, a], e_ch + 6 + a, dn_face)
        arrive(kv.at[8 - base + (z + 4) % 8, a], e_ch + a, facing)

    def head_step(a, _):
        crossed(a)
        remote_unit(0, a)

        @pl.when(a == 0)
        def _():
            do(second_z, 2)
            do(ring, 4, 1)

        @pl.when(a == 1)
        def _():
            do(ring, 4, 2)

        remote_unit(1, a)

        @pl.when(a == 0)
        def _():
            do(ring, 3, 2)
            do(weight_x2, 7)
            do(second_z, 3)

        @pl.when(a > 0)
        def _():
            finish(a - 1)

        @pl.when(a == 1)
        def _():
            do(second_z, 4)

        @pl.when(a == 2)
        def _():
            relay_near(0)

        own_unit(a)

        return 0

    lax.fori_loop(0, HEADS_DEV, head_step, 0)
    relay_near(1)
    finish(HEADS_DEV - 1)
    relay_far(0)
    relay_far(1)
    for n in range(8):
        arrive(wb.at[xf, z_of(n)], x2_ch + n)
    arrive(wf, wy_ch)
    relay_near(2)
    eight, four = ab.at[pl.ds(0, 8)], ab.at[pl.ds(0, 4)]
    copy(eight, eight, c_ch, z_up).wait_recv()

    def wide(gg, heads):
        return jnp.concatenate([ab[HEADS_DEV * gg + a] for a in heads], axis=1)

    def project(half, heads):
        rows_at = slice(heads[0] * HD, (heads[-1] + 1) * HD)
        acc = jnp.zeros((TILE, WIDTH), jnp.float32)
        for j in range(4):
            for k in range(2):
                if half == 0:
                    left, rows = wide(4 * k + j, heads), wb[j, :, k]
                elif k == 0:
                    left, rows = wide(4 * y + j, heads), w2[:, j]
                else:
                    left, rows = wide(4 - 4 * y + j, heads), wf[:, j]
                acc = acc + jnp.dot(left, rows.reshape(WIDTH, WIDTH)[rows_at], preferred_element_type=jnp.float32)
        return acc

    for half in range(2):
        part_sum[half] = project(half, (0, 1))
    relay_far(2)
    copy(four, four, c_ch + 1, z_up).wait_recv()
    for half in range(2):
        total = part_sum[half] + project(half, (2,))
        out_ref[:, half * WIDTH : (half + 1) * WIDTH] = total.astype(jnp.bfloat16)

    draining[0] = True
    for step, which in done:
        step(*which)
    for a in range(HEADS_DEV):
        for i, cond, dev in edge:
            for c in back(i - 1, a, dev):
                pl.when(cond)(c.wait_send)
        for c in near(g, g, a) + halves(lower, upper, a):
            c.wait_send()
    copy(eight, eight, c_ch, partner).wait_send()
    copy(four, four, c_ch + 1, partner).wait_send()
    copy(wf, wf, wy_ch, y_flip).wait_send()
    sevenths = qb.at[0, pl.ds(0, 224)]
    copy(sevenths, sevenths, q_ch, partner).wait_send()
    assert channels[0] == N_CH, channels[0]


def local(queries, keys, values, window, out_weight):
    any_spec = pl.BlockSpec(memory_space=pl.ANY)
    bf16, f32 = jnp.bfloat16, jnp.float32
    return pl.pallas_call(
        kernel,
        out_shape=jax.ShapeDtypeStruct((TILE, out_weight.shape[1]), bf16),
        in_specs=[any_spec] * 3 + [pl.BlockSpec(memory_space=pltpu.SMEM), any_spec],
        out_specs=pl.BlockSpec(memory_space=pltpu.VMEM),
        scratch_shapes=[
            pltpu.VMEM((16, HEADS_DEV, 2, TILE, HD), bf16),
            pltpu.VMEM((4, 8, 2, 48, WIDTH), bf16),
            pltpu.VMEM((8, 4, 48, WIDTH), bf16),
            pltpu.VMEM((8, 4, 48, WIDTH), bf16),
            pltpu.VMEM((3, TILE, WIDTH), bf16),
            pltpu.VMEM((3, 32, HD), f32),
            pltpu.VMEM((GROUPS * HEADS_DEV, TILE, HD), bf16),
            pltpu.VMEM((9, TILE, TILE), f32),
            pltpu.VMEM((2, HEADS_DEV, TILE, HD), bf16),
            pltpu.VMEM((2, HEADS_DEV, 8, TILE), f32),
            pltpu.VMEM((2, HEADS_DEV, TILE, HD), bf16),
            pltpu.VMEM((2, HEADS_DEV, 8, TILE), f32),
            pltpu.VMEM((2, TILE, 2 * HD), f32),
            pltpu.VMEM((2, TILE, HD), f32),
            pltpu.VMEM((2, TILE, WIDTH), f32),
            pltpu.SemaphoreType.DMA((N_CH,)),
            pltpu.SemaphoreType.DMA((N_CH,)),
            pltpu.SemaphoreType.DMA((9,)),
        ],
        compiler_params=pltpu.CompilerParams(
            collective_id=0, has_side_effects=True, vmem_limit_bytes=60 * 1024 * 1024),
    )(queries, keys, values, window, out_weight)


def solution(mesh):
    in_specs = (
        P(("seq", "head"), None),
        P("seq", "head"),
        P("seq", "head"),
        P("seq", None),
        P("seq", "head"),
    )
    return jax.shard_map(local, mesh=mesh, in_specs=in_specs, out_specs=P("seq", "head"), check_vma=False)
```
